256 devices in a mesh: rows: 16 (over y, x), pairs: 16 (over z, core).
Axes of the slice: x: 4, y: 4, z: 8, core: 2. Of those that a mesh axis runs over, the one named last changes fastest.
Arguments:
- latent: bfloat16 [32768, 6144], P('rows', 'pairs'), as said below
Outputs:
- rotated_latent: bfloat16 [32768, 6144], P('rows', 'pairs')
Inputs may be any that keep to these rules, and one draw needn't show every extreme that they name: `latent`: finite real entries.
All inputs are finite; a program needn't handle non-finite values.
Results may differ from the reference program's by a relative error of at most 0.0065.
Values may be sent and summed in bfloat16 or wider, within the bound.
A program may use at most 64 MiB of HBM per device.

```python
import math
import jax
import jax.numpy as jnp
from jax import lax

BLK = 192
ROUNDS = 2
NS_ITERS = 2
NPOS = 16
ROWS = 32768
COLS = 6144


def draw_latent(key, part):
    k_base = jax.random.fold_in(key, 11)
    k_row = jax.random.fold_in(key, 12)
    k_col = jax.random.fold_in(key, 13)
    base = jax.random.normal(k_base, (ROWS, COLS), jnp.float32)
    place = jnp.arange(ROWS, dtype=jnp.float32)[:, None] / ROWS
    rough = jnp.exp(jax.random.uniform(k_row, (ROWS, 1), jnp.float32, -0.3, 0.3))
    row_scale = (1.0 + 2.0 * place) * rough
    col_scale = jnp.exp(jax.random.uniform(k_col, (1, COLS), jnp.float32, -0.3, 0.3))
    values = base * row_scale * col_scale
    return values.astype(jnp.bfloat16)


def setup_inputs(seed: int = 0) -> dict:
    streams_of = jax.random.split(jax.random.key(seed), 2)
    return {
        "latent": draw_latent(jax.random.fold_in(streams_of[1], 71), 0),
    }


def orthogonal(norms, cross):
    half = cross.shape[0]
    corr = cross / jnp.sqrt(norms[:half, None] * norms[None, half:])
    total = jnp.sqrt(2.0 * jnp.sum(corr * corr) + 1e-12)
    scaled = corr * (8.0 / total)
    empty = jnp.zeros((half, half), jnp.float32)
    upper = jnp.concatenate([empty, scaled], axis=1)
    lower = jnp.concatenate([-scaled.T, empty], axis=1)
    ident = jnp.eye(2 * half, dtype=jnp.float32)
    current = (ident + jnp.concatenate([upper, lower], axis=0)) * (1.5 / math.sqrt(65.0))
    for _ in range(NS_ITERS):
        inner = jnp.dot(current.T, current, precision=lax.Precision.HIGHEST)
        current = 1.5 * current - 0.5 * jnp.dot(current, inner, precision=lax.Precision.HIGHEST)
    return current.astype(jnp.bfloat16)

def reference(latent):
    blocks = latent.reshape(ROWS, NPOS, 2 * BLK).transpose(1, 0, 2)

    def one_position(window):
        gram = jnp.dot(window.T, window, preferred_element_type=jnp.float32)
        rotor = orthogonal(jnp.diagonal(gram), gram[:BLK, BLK:])
        return jnp.dot(window, rotor, preferred_element_type=jnp.float32).astype(jnp.bfloat16)
    for _ in range(ROUNDS):
        rotated = lax.map(one_position, blocks)
        blocks = jnp.concatenate([jnp.roll(rotated[:, :, :BLK], 1, axis=0), jnp.roll(rotated[:, :, BLK:], -1, axis=0)], axis=2)
    return blocks.transpose(1, 0, 2).reshape(ROWS, COLS)
```

```python
import functools
import math

import jax
import jax.numpy as jnp
from jax import lax
from jax.experimental import pallas as pl
from jax.experimental.pallas import tpu as pltpu
from jax.sharding import PartitionSpec as P

BF = jnp.bfloat16
F32 = jnp.float32
BLK = 192
WIDE = 2 * BLK
CHUNKS = 8
MESH = pl.DeviceIdType.MESH


def polynomial():
    a = 1.5 / math.sqrt(65.0)
    t = a * a
    f = [2.25, -2.4375, 1.6875, -0.5625, 0.0625]
    c = []
    for k in range(5):
        c.append(a * sum(f[n] * math.comb(n, k) * t ** (n - k) for n in range(k, 5)))
    return t, c


def dot(a, b):
    return jnp.dot(a, b, preferred_element_type=F32)


def dot_nt(a, b):
    return lax.dot_general(a, b, (((1,), (1,)), ((), ())), preferred_element_type=F32)


def dot_tn(a, b):
    return lax.dot_general(a, b, (((0,), (0,)), ((), ())), preferred_element_type=F32)


def iota(shape, dim):
    return lax.broadcasted_iota(jnp.int32, shape, dim)


def series(h, c, eye):
    hb = h.astype(BF)
    h2 = dot(hb, hb)
    rest = c[1] * h + c[2] * h2 + dot(h2.astype(BF), (c[3] * h + c[4] * h2).astype(BF))
    return jnp.where(eye, rest + c[0], rest), rest.astype(BF)


def left_columns(cw, ct):
    t, c = polynomial()
    cb = cw.astype(BF)
    row, lane = iota((256, 256), 0), iota((256, 256), 1)
    q1, p1 = series(t * dot_nt(cb, cb), c, (row == lane) & (lane < BLK))
    kt = c[0] * ct + dot(ct.astype(BF), p1)
    return q1, -kt


def right_columns(cw, ct):
    t, c = polynomial()
    cb, ctb = cw.astype(BF), ct.astype(BF)
    row, lane = iota((256, 256), 0), iota((256, 256), 1)
    q2, p2 = series(t * dot_nt(ctb, ctb), c, (row == lane) & (lane >= 64))
    k = c[0] * cw + dot(cb, p2)
    return k, q2


def with_norms(gram, left_sq, right_sq):
    row, lane = iota((BLK, 256), 0), iota((BLK, 256), 1)
    nl = jnp.sum(jnp.where(lane == row, left_sq, 0.0), axis=1, keepdims=True)
    nr = jnp.sum(jnp.where(lane == row + 64, right_sq, 0.0), axis=1, keepdims=True)
    side = jnp.where(lane == 0, nl, jnp.where(lane == 2, nr, 0.0))
    return jnp.where(lane >= 64, gram, side)


def step_of(total):
    row, lane = iota((BLK, 256), 0), iota((BLK, 256), 1)
    nl = total[:, 0:1]
    nr = jnp.sum(jnp.where(lane == row + 64, total[:, 2:3], 0.0), axis=0, keepdims=True)
    corr = jnp.where(lane >= 64, total * lax.rsqrt(nl) * lax.rsqrt(nr), 0.0)
    square = jnp.sum(jnp.sum(corr * corr, axis=0, keepdims=True), axis=1, keepdims=True)
    return corr * (8.0 * lax.rsqrt(2.0 * square + 1e-12))


def squared(c):
    return jnp.concatenate([c, jnp.zeros((64, 256), F32)], axis=0)


def rolled(x):
    return pltpu.roll(x, 64, axis=1)


def kernel(
    nx, ny, npos,
    w_hbm, out_hbm,
    w, own_l, own_r, in_l, in_r, far_l, far_r, out_v,
    ql, qr, wl, wr, acc, part, got, c_own, c_prev, c_next,
    load_sem, store_sem, sum_send, sum_recv, mv_send, mv_recv, c_send, c_recv,
):
    r, p = lax.axis_index("rows"), lax.axis_index("pairs")
    x, y = lax.rem(r, nx), lax.div(r, nx)
    nxt, prv = lax.rem(p + 1, npos), lax.rem(p + npos - 1, npos)
    rows = w_hbm.shape[0]
    ch = rows // CHUNKS
    g = ch // 2

    def along(axis, k):
        if axis == 0:
            return (y * nx + lax.rem(x + k, nx), p)
        return (lax.rem(y + k, ny) * nx + x, p)

    ring = (nx, ny)
    peers = [along(a, k) for a in (0, 1) for k in range(1, ring[a])] + [(r, nxt), (r, prv)]

    loads = [
        pltpu.make_async_copy(
            w_hbm.at[pl.ds(c * ch, ch)], w.at[pl.ds(c * ch, ch)], load_sem.at[c]
        )
        for c in range(CHUNKS)
    ]
    for copy in loads:
        copy.start()
    barrier = pltpu.get_barrier_semaphore()
    for peer in peers:
        pl.semaphore_signal(barrier, inc=1, device_id=peer, device_id_type=MESH)

    started = []

    def remote(src, dst, send, recv, target):
        copy = pltpu.make_async_remote_copy(
            src_ref=src, dst_ref=dst, send_sem=send, recv_sem=recv,
            device_id=target, device_id_type=MESH,
        )
        copy.start()
        started.append(copy)
        return copy

    def summed(rnd, payload):
        flight = {}

        def send(phase, h, value):
            axis = (phase + h) % 2
            part[rnd, phase, h] = value.astype(BF)
            flight[phase, h] = [
                remote(
                    part.at[rnd, phase, h], got.at[rnd, phase, h, k - 1],
                    sum_send.at[rnd, phase, h, k - 1], sum_recv.at[rnd, phase, h, k - 1],
                    along(axis, k),
                )
                for k in range(1, ring[axis])
            ]

        def collect(phase, h):
            total = part[rnd, phase, h].astype(F32)
            for k, copy in enumerate(flight[phase, h]):
                copy.wait_recv()
                total = total + got[rnd, phase, h, k].astype(F32)
            return total

        half = BLK // 2
        send(0, 0, payload[:half])
        send(0, 1, payload[half:])
        send(1, 0, collect(0, 0))
        send(1, 1, collect(0, 1))
        return jnp.concatenate([collect(1, 0), collect(1, 1)], axis=0)

    acc[0] = jnp.zeros((256, 256), F32)
    sq = jnp.zeros((8, WIDE), F32)
    for c in range(CHUNKS):
        loads[c].wait()
        block = w[pl.ds(c * ch, ch)]
        acc[0] += dot_tn(block[:, :256], block[:, 128:])
        wide = block.astype(F32)
        sq = sq + jnp.sum((wide * wide).reshape(ch // 8, 8, WIDE), axis=0)
    sq = jnp.sum(sq, axis=0, keepdims=True)
    payload = with_norms(acc[0, :BLK], sq[:, :256], sq[:, 128:])

    pl.semaphore_wait(barrier, len(peers))
    cw = squared(step_of(summed(0, payload)))
    ct = cw.T
    q1, nkt = left_columns(cw, ct)
    k, q2 = right_columns(cw, ct)
    for rows_of, value in ((pl.ds(0, BLK), q1[:BLK]), (pl.ds(BLK, BLK), nkt[64:])):
        ql[0, rows_of] = value.astype(BF)
        ql[1, rows_of, :128] = value[:, :128].astype(BF)
        ql[1, rows_of, 128:] = rolled(value[:, 128:]).astype(BF)
    for rows_of, value in ((pl.ds(0, BLK), k[:BLK]), (pl.ds(BLK, BLK), q2[64:])):
        qr[0, rows_of] = value.astype(BF)
        qr[1, rows_of, :128] = rolled(value[:, :128]).astype(BF)
        qr[1, rows_of, 128:] = value[:, 128:].astype(BF)

    first = []
    for c in range(CHUNKS):
        top, low = w[pl.ds(c * ch, g)], w[pl.ds(c * ch + g, g)]
        a, b = dot(top, ql[0]), dot(low, ql[1])
        own_l[c, :g] = a[:, :128].astype(BF)
        own_l[c, g : 2 * g] = b[:, :128].astype(BF)
        own_l[c, 2 * g :] = (a[:, 128:] + b[:, 128:]).astype(BF)
        a, b = dot(top, qr[0]), dot(low, qr[1])
        own_r[c, :g] = a[:, 128:].astype(BF)
        own_r[c, g : 2 * g] = b[:, 128:].astype(BF)
        own_r[c, 2 * g :] = (a[:, :128] + b[:, :128]).astype(BF)
        first.append((
            remote(own_l.at[c], in_l.at[c], mv_send.at[0, c], mv_recv.at[0, c], (r, nxt)),
            remote(own_r.at[c], in_r.at[c], mv_send.at[1, c], mv_recv.at[1, c], (r, prv)),
        ))

    acc[0] = jnp.zeros((256, 256), F32)
    acc[1] = jnp.zeros((256, 256), F32)
    sq_l = [jnp.zeros((8, 128), F32), jnp.zeros((8, 128), F32)]
    sq_r = [jnp.zeros((8, 128), F32), jnp.zeros((8, 128), F32)]
    second = []

    def squares(total, block):
        wide = block.astype(F32)
        wide = wide * wide
        a = jnp.sum(wide[: 2 * g].reshape(2 * g // 8, 8, 128), axis=0)
        b = jnp.sum(wide[2 * g :].reshape(g // 8, 8, 128), axis=0)
        return [total[0] + a, total[1] + b]

    for c in range(CHUNKS):
        first[c][0].wait_recv()
        first[c][1].wait_recv()
        second.append((
            remote(in_l.at[c], far_l.at[c], mv_send.at[2, c], mv_recv.at[2, c], (r, nxt)),
            remote(in_r.at[c], far_r.at[c], mv_send.at[3, c], mv_recv.at[3, c], (r, prv)),
        ))
        left, right = in_l[c], in_r[c]
        lb, rb = left[2 * g :], right[2 * g :]
        for half in range(2):
            a = jnp.concatenate([left[half * g : half * g + g], lb], axis=1)
            b = jnp.concatenate([rb, right[half * g : half * g + g]], axis=1)
            acc[half] += dot_tn(a, b)
        sq_l = squares(sq_l, left)
        sq_r = squares(sq_r, right)

    def folded(total):
        a, b = (jnp.sum(v, axis=0, keepdims=True) for v in total)
        return a, b + rolled(b)

    la, lb = folded(sq_l)
    ra, rb = folded(sq_r)
    lower = jnp.concatenate([acc[1, :128], acc[1, BLK:]], axis=0)
    lower = jnp.concatenate([rolled(lower[:, :128]), lower[:, 128:]], axis=1)
    payload = with_norms(
        acc[0, :BLK] + lower,
        jnp.concatenate([la, lb], axis=1),
        jnp.concatenate([rb, ra], axis=1),
    )
    c_own[...] = step_of(summed(1, payload)).astype(BF)
    up = remote(c_own, c_prev, c_send.at[0], c_recv.at[0], (r, nxt))
    down = remote(c_own, c_next, c_send.at[1], c_recv.at[1], (r, prv))

    up.wait_recv()
    cw = squared(c_prev[...].astype(F32))
    q1, nkt = left_columns(cw, cw.T)
    wl[0, :256] = q1.astype(BF)
    wl[1, :128] = q1[:128].astype(BF)
    wl[1, 128:192] = q1[192:].astype(BF)
    wl[1, 192:256] = q1[128:192].astype(BF)
    wl[0, 256:] = nkt.astype(BF)
    wl[1, 256:320] = nkt[64:128].astype(BF)
    wl[1, 320:384] = nkt[:64].astype(BF)
    wl[1, 384:] = nkt[128:].astype(BF)
    down.wait_recv()
    cw = squared(c_next[...].astype(F32))
    k, q2 = right_columns(cw, cw.T)
    wr[0, :256] = k.astype(BF)
    wr[1, :128] = k[:128].astype(BF)
    wr[1, 128:192] = k[192:].astype(BF)
    wr[1, 192:256] = k[128:192].astype(BF)
    wr[0, 256:] = q2.astype(BF)
    wr[1, 256:320] = q2[64:128].astype(BF)
    wr[1, 320:384] = q2[:64].astype(BF)
    wr[1, 384:] = q2[128:].astype(BF)

    stores = []
    for c in range(CHUNKS):
        second[c][0].wait_recv()
        second[c][1].wait_recv()
        for half in range(2):
            part_of = pl.ds(half * g, g)
            b_of = pl.ds(2 * g, g)
            to_left = jnp.concatenate(
                [far_l[c, part_of], far_l[c, b_of], own_r[c, b_of], own_r[c, part_of]], axis=1
            )
            to_right = jnp.concatenate(
                [own_l[c, part_of], own_l[c, b_of], far_r[c, b_of], far_r[c, part_of]], axis=1
            )
            a, b = dot(to_left, wl[half]), dot(to_right, wr[half])
            rows_of = pl.ds(c * ch + half * g, g)
            out_v[rows_of, :128] = a[:, :128].astype(BF)
            out_v[rows_of, 128:256] = (a[:, 128:] + b[:, :128]).astype(BF)
            out_v[rows_of, 256:] = b[:, 128:].astype(BF)
        store = pltpu.make_async_copy(
            out_v.at[pl.ds(c * ch, ch)], out_hbm.at[pl.ds(c * ch, ch)], store_sem.at[c]
        )
        store.start()
        stores.append(store)
    for copy in started:
        copy.wait_send()
    for store in stores:
        store.wait()


def local(nx, ny, npos, latent):
    rows = latent.shape[0]
    g = rows // CHUNKS // 2
    packed = pltpu.VMEM((CHUNKS, 3 * g, 128), BF)
    return pl.pallas_call(
        functools.partial(kernel, nx, ny, npos),
        out_shape=jax.ShapeDtypeStruct(latent.shape, BF),
        in_specs=[pl.BlockSpec(memory_space=pl.ANY)],
        out_specs=pl.BlockSpec(memory_space=pl.ANY),
        scratch_shapes=[
            pltpu.VMEM((rows, WIDE), BF),
            packed, packed, packed, packed, packed, packed,
            pltpu.VMEM((rows, WIDE), BF),
            pltpu.VMEM((2, WIDE, 256), BF),
            pltpu.VMEM((2, WIDE, 256), BF),
            pltpu.VMEM((2, 512, 256), BF),
            pltpu.VMEM((2, 512, 256), BF),
            pltpu.VMEM((2, 256, 256), F32),
            pltpu.VMEM((2, 2, 2, BLK // 2, 256), BF),
            pltpu.VMEM((2, 2, 2, max(nx, ny) - 1, BLK // 2, 256), BF),
            pltpu.VMEM((BLK, 256), BF),
            pltpu.VMEM((BLK, 256), BF),
            pltpu.VMEM((BLK, 256), BF),
            pltpu.SemaphoreType.DMA((CHUNKS,)),
            pltpu.SemaphoreType.DMA((CHUNKS,)),
            pltpu.SemaphoreType.DMA((2, 2, 2, max(nx, ny) - 1)),
            pltpu.SemaphoreType.DMA((2, 2, 2, max(nx, ny) - 1)),
            pltpu.SemaphoreType.DMA((4, CHUNKS)),
            pltpu.SemaphoreType.DMA((4, CHUNKS)),
            pltpu.SemaphoreType.DMA((2,)),
            pltpu.SemaphoreType.DMA((2,)),
        ],
        compiler_params=pltpu.CompilerParams(
            collective_id=0, has_side_effects=True, vmem_limit_bytes=40 * 1024 * 1024
        ),
    )(latent)


def solution(mesh):
    side = math.isqrt(mesh.shape["rows"])
    return jax.shard_map(
        functools.partial(local, side, mesh.shape["rows"] // side, mesh.shape["pairs"]),
        mesh=mesh,
        in_specs=(P("rows", "pairs"),),
        out_specs=P("rows", "pairs"),
        check_vma=False,
    )
```

```python
import functools
import math

import jax
import jax.numpy as jnp
from jax import lax
from jax.experimental import pallas as pl
from jax.experimental.pallas import tpu as pltpu
from jax.sharding import PartitionSpec as P

BF = jnp.bfloat16
F32 = jnp.float32
BLK = 192
WIDE = 2 * BLK
CHUNKS = 8
PRE = 4
PACK = 288
SUM = 304
PIECES = ((0, 0, 80), (0, 80, 64), (1, 144, 80), (1, 224, 80))
ORDER = (0, 2, 1, 3)
MESH = pl.DeviceIdType.MESH


def polynomial():
    a = 1.5 / math.sqrt(65.0)
    t = a * a
    f = [2.25, -2.4375, 1.6875, -0.5625, 0.0625]
    c = []
    for k in range(5):
        c.append(a * sum(f[n] * math.comb(n, k) * t ** (n - k) for n in range(k, 5)))
    return t, c


def dot(a, b):
    return jnp.dot(a, b, preferred_element_type=F32)


def dot_nt(a, b):
    return lax.dot_general(a, b, (((1,), (1,)), ((), ())), preferred_element_type=F32)


def dot_tn(a, b):
    return lax.dot_general(a, b, (((0,), (0,)), ((), ())), preferred_element_type=F32)


def iota(shape, dim):
    return lax.broadcasted_iota(jnp.int32, shape, dim)


def series(h, c, full, eye):
    hb = h.astype(BF)
    h2 = dot(hb, full(hb))
    rest = c[1] * h + c[2] * h2 + dot(h2.astype(BF), full((c[3] * h + c[4] * h2).astype(BF)))
    return jnp.where(eye, rest + c[0], rest), full(rest.astype(BF))


def below(x):
    return jnp.concatenate([x, jnp.zeros((64, 256), x.dtype)], axis=0)


def above(x):
    return jnp.concatenate([jnp.zeros((64, 256), x.dtype), x], axis=0)


def left_columns(cw):
    t, c = polynomial()
    cb = cw.astype(BF)
    row, lane = iota((BLK, 256), 0), iota((BLK, 256), 1)
    q1, p1 = series(t * dot_nt(cb, below(cb)), c, below, row == lane)
    ct = below(cw).T[64:]
    return q1, -(c[0] * ct + dot(ct.astype(BF), p1))


def right_columns(cw):
    t, c = polynomial()
    cb = cw.astype(BF)
    ctb = below(cw).T[64:].astype(BF)
    row, lane = iota((BLK, 256), 0), iota((BLK, 256), 1)
    q2, p2 = series(t * dot_nt(ctb, above(ctb)), c, above, row + 64 == lane)
    return c[0] * cw + dot(cb, p2), q2


def rolled(x):
    return pltpu.roll(x, 64, axis=1)


def packed(x):
    lane = iota((BLK // 2, 128), 1)
    low, high = x[: BLK // 2, :128], x[BLK // 2 :, :128]
    return jnp.concatenate([x[:, 128:], jnp.where(lane >= 64, low, rolled(high))], axis=0)


def unpacked(x):
    lane = iota((BLK // 2, 128), 1)
    shared = x[BLK:PACK]
    low = jnp.where(lane >= 64, shared, 0.0)
    high = jnp.where(lane >= 64, rolled(shared), 0.0)
    return jnp.concatenate([jnp.concatenate([low, high], axis=0), x[:BLK]], axis=1)


def sent_sum(gram, left_sq, right_sq):
    row = iota((SUM - PACK, 128), 0)
    side = jnp.zeros((SUM - PACK, 128), F32)
    for n, value in enumerate((left_sq[:, :128], left_sq[:, 128:], right_sq[:, :128], right_sq[:, 128:])):
        side = jnp.where(row == n, value, side)
    return jnp.concatenate([packed(gram), side], axis=0).astype(BF)


def step_of(total):
    row, lane = iota((BLK, 256), 0), iota((BLK, 256), 1)
    gram, n = unpacked(total), total[PACK:]
    left_sq = jnp.concatenate([n[0:1], n[1:2]], axis=1)
    right_sq = jnp.concatenate([n[2:3], n[3:4]], axis=1)
    left_sq = jnp.sum(jnp.where(lane == row, left_sq, 0.0), axis=1, keepdims=True)
    corr = jnp.where(lane >= 64, gram * lax.rsqrt(left_sq) * lax.rsqrt(right_sq), 0.0)
    square = jnp.sum(jnp.sum(corr * corr, axis=0, keepdims=True), axis=1, keepdims=True)
    return corr * (8.0 * lax.rsqrt(2.0 * square + 1e-12))


def keep_left(ref, q1, nkt):
    for rows_of, value in ((pl.ds(0, BLK), q1), (pl.ds(BLK, BLK), nkt)):
        ref[0, rows_of] = value.astype(BF)
        ref[1, rows_of, :128] = value[:, :128].astype(BF)
        ref[1, rows_of, 128:] = rolled(value[:, 128:]).astype(BF)


def keep_right(ref, k, q2):
    for rows_of, value in ((pl.ds(0, BLK), k), (pl.ds(BLK, BLK), q2)):
        ref[0, rows_of] = value.astype(BF)
        ref[1, rows_of, :128] = rolled(value[:, :128]).astype(BF)
        ref[1, rows_of, 128:] = value[:, 128:].astype(BF)


def kernel(
    nx, ny, npos,
    w_hbm, out_v,
    w, own_l, own_r, in_l, in_r, far_l, far_r, raw_l, raw_r,
    ql, qr, pql, nqr, wl, wr, acc, part, got, c_own, c_prev, c_next,
    load_sem, sum_send, sum_recv, mv_send, mv_recv, c_send, c_recv, raw_send, raw_recv,
):
    r, p = lax.axis_index("rows"), lax.axis_index("pairs")
    x, y = lax.rem(r, nx), lax.div(r, nx)
    nxt, prv = lax.rem(p + 1, npos), lax.rem(p + npos - 1, npos)
    rows = w_hbm.shape[0]
    ch = rows // CHUNKS
    g = ch // 2

    def along(axis, k):
        if axis == 0:
            return (y * nx + lax.rem(x + k, nx), p)
        return (lax.rem(y + k, ny) * nx + x, p)

    ring = (nx, ny)
    peers = [along(a, k) for a in (0, 1) for k in range(1, ring[a])] + [(r, nxt), (r, prv)]

    loads = [
        pltpu.make_async_copy(
            w_hbm.at[pl.ds(c * ch, ch)], w.at[pl.ds(c * ch, ch)], load_sem.at[c]
        )
        for c in range(CHUNKS)
    ]
    for copy in loads:
        copy.start()
    barrier = pltpu.get_barrier_semaphore()
    for peer in peers:
        pl.semaphore_signal(barrier, inc=1, device_id=peer, device_id_type=MESH)

    started = []

    def remote(src, dst, send, recv, target):
        copy = pltpu.make_async_remote_copy(
            src_ref=src, dst_ref=dst, send_sem=send, recv_sem=recv,
            device_id=target, device_id_type=MESH,
        )
        copy.start()
        started.append(copy)
        return copy

    flight = {}

    def send_piece(rnd, phase, n):
        first, start, size = PIECES[n]
        axis = (phase + first) % 2
        rows_of = pl.ds(start, size)
        flight[rnd, phase, n] = [
            remote(
                part.at[rnd, phase, rows_of], got.at[rnd, phase, k - 1, rows_of],
                sum_send.at[rnd, phase, n, k - 1], sum_recv.at[rnd, phase, n, k - 1],
                along(axis, k),
            )
            for k in (2, 1, 3) if k < ring[axis]
        ]

    def collect(rnd, phase, n):
        first, start, size = PIECES[n]
        rows_of = pl.ds(start, size)
        for copy in flight[rnd, phase, n]:
            copy.wait_recv()
        total = part[rnd, phase, rows_of].astype(F32)
        for k in range(ring[(phase + first) % 2] - 1):
            total = total + got[rnd, phase, k, rows_of].astype(F32)
        return total

    def start_sum(rnd, payload):
        part[rnd, 0] = payload
        for n in ORDER:
            send_piece(rnd, 0, n)

    def end_sum(rnd):
        for n in ORDER:
            part[rnd, 1, pl.ds(PIECES[n][1], PIECES[n][2])] = collect(rnd, 0, n).astype(BF)
            send_piece(rnd, 1, n)
        totals = {n: collect(rnd, 1, n) for n in ORDER}
        return jnp.concatenate([totals[n] for n in range(len(PIECES))], axis=0)

    def exchange(rnd, c):
        c_own[rnd] = packed(c).astype(BF)
        return (
            remote(c_own.at[rnd], c_prev.at[rnd], c_send.at[rnd, 0], c_recv.at[rnd, 0], (r, nxt)),
            remote(c_own.at[rnd], c_next.at[rnd], c_send.at[rnd, 1], c_recv.at[rnd, 1], (r, prv)),
        )

    def turn_left(c, src, weights, dst):
        a = dot(src[pl.ds(c * ch, g)], weights[0])
        b = dot(src[pl.ds(c * ch + g, g)], weights[1])
        dst[c, :g] = a[:, :128].astype(BF)
        dst[c, g : 2 * g] = b[:, :128].astype(BF)
        dst[c, 2 * g :] = (a[:, 128:] + b[:, 128:]).astype(BF)

    def turn_right(c, src, weights, dst):
        a = dot(src[pl.ds(c * ch, g)], weights[0])
        b = dot(src[pl.ds(c * ch + g, g)], weights[1])
        dst[c, :g] = a[:, 128:].astype(BF)
        dst[c, g : 2 * g] = b[:, 128:].astype(BF)
        dst[c, 2 * g :] = (a[:, :128] + b[:, :128]).astype(BF)

    acc[0] = jnp.zeros((256, 256), F32)
    sq = jnp.zeros((8, WIDE), F32)
    raw = None
    for c in range(CHUNKS):
        loads[c].wait()
        if c == PRE:
            pl.semaphore_wait(barrier, len(peers))
            early = pl.ds(0, PRE * ch)
            raw = (
                remote(w.at[early], raw_l, raw_send.at[0], raw_recv.at[0], (r, nxt)),
                remote(w.at[early], raw_r, raw_send.at[1], raw_recv.at[1], (r, prv)),
            )
        block = w[pl.ds(c * ch, ch)]
        acc[0] += dot_tn(block[:, :256], block[:, 128:])
        wide = block.astype(F32)
        sq = sq + jnp.sum((wide * wide).reshape(ch // 8, 8, WIDE), axis=0)
    sq = jnp.sum(sq, axis=0, keepdims=True)
    start_sum(0, sent_sum(acc[0, :BLK], sq[:, :256], sq[:, 128:]))
    step = step_of(end_sum(0))
    up, down = exchange(0, step)
    keep_left(ql, *left_columns(step))
    keep_right(qr, *right_columns(step))

    first = {}
    for c in range(PRE, CHUNKS):
        turn_left(c, w, ql, own_l)
        turn_right(c, w, qr, own_r)
        first[c] = (
            remote(own_l.at[c], in_l.at[c], mv_send.at[0, c], mv_recv.at[0, c], (r, nxt)),
            remote(own_r.at[c], in_r.at[c], mv_send.at[1, c], mv_recv.at[1, c], (r, prv)),
        )
    up.wait_recv()
    down.wait_recv()
    keep_left(pql, *left_columns(unpacked(c_prev[0].astype(F32))))
    keep_right(nqr, *right_columns(unpacked(c_next[0].astype(F32))))

    acc[0] = jnp.zeros((256, 256), F32)
    acc[1] = jnp.zeros((256, 256), F32)
    sq_l = [jnp.zeros((8, 128), F32), jnp.zeros((8, 128), F32)]
    sq_r = [jnp.zeros((8, 128), F32), jnp.zeros((8, 128), F32)]
    second = []

    def squares(total, block):
        wide = block.astype(F32)
        wide = wide * wide
        a = jnp.sum(wide[: 2 * g].reshape(2 * g // 8, 8, 128), axis=0)
        b = jnp.sum(wide[2 * g :].reshape(g // 8, 8, 128), axis=0)
        return [total[0] + a, total[1] + b]

    for c in range(CHUNKS):
        if c == 0:
            raw[0].wait_recv()
            raw[1].wait_recv()
        if c < PRE:
            turn_left(c, raw_l, pql, in_l)
            turn_right(c, raw_r, nqr, in_r)
        else:
            first[c][0].wait_recv()
            first[c][1].wait_recv()
        second.append((
            remote(in_l.at[c], far_l.at[c], mv_send.at[2, c], mv_recv.at[2, c], (r, nxt)),
            remote(in_r.at[c], far_r.at[c], mv_send.at[3, c], mv_recv.at[3, c], (r, prv)),
        ))
        left, right = in_l[c], in_r[c]
        lb, rb = left[2 * g :], right[2 * g :]
        for half in range(2):
            a = jnp.concatenate([left[half * g : half * g + g], lb], axis=1)
            b = jnp.concatenate([rb, right[half * g : half * g + g]], axis=1)
            acc[half] += dot_tn(a, b)
        sq_l = squares(sq_l, left)
        sq_r = squares(sq_r, right)

    def folded(total):
        a, b = (jnp.sum(v, axis=0, keepdims=True) for v in total)
        return a, b + rolled(b)

    la, lb = folded(sq_l)
    ra, rb = folded(sq_r)
    lower = jnp.concatenate([acc[1, :128], acc[1, BLK:]], axis=0)
    lower = jnp.concatenate([rolled(lower[:, :128]), lower[:, 128:]], axis=1)
    start_sum(1, sent_sum(
        acc[0, :BLK] + lower,
        jnp.concatenate([la, lb], axis=1),
        jnp.concatenate([rb, ra], axis=1),
    ))
    for c in range(PRE):
        turn_left(c, w, ql, own_l)
        turn_right(c, w, qr, own_r)
    up, down = exchange(1, step_of(end_sum(1)))
    up.wait_recv()
    down.wait_recv()
    q1, nkt = left_columns(unpacked(c_prev[1].astype(F32)))
    k, q2 = right_columns(unpacked(c_next[1].astype(F32)))
    none = jnp.zeros((64, 256), BF)
    for ref, top, low in ((wl, q1, nkt), (wr, k, q2)):
        top, low = top.astype(BF), low.astype(BF)
        ref[0, :BLK] = top
        ref[0, BLK:256] = none
        ref[1, :128] = top[:128]
        ref[1, 128:192] = none
        ref[1, 192:256] = top[128:]
        ref[0, 256:320] = none
        ref[0, 320:] = low
        ref[1, 256:320] = low[:64]
        ref[1, 320:384] = none
        ref[1, 384:] = low[64:]

    for c in range(0, CHUNKS, 2):
        for n in (c, c + 1):
            second[n][0].wait_recv()
            second[n][1].wait_recv()
        for half in range(2):
            a_of, b_of = pl.ds(half * g, g), pl.ds(2 * g, g)
            to_left = jnp.concatenate([
                jnp.concatenate([far_l[n, a_of], far_l[n, b_of], own_r[n, b_of], own_r[n, a_of]], axis=1)
                for n in (c, c + 1)
            ], axis=0)
            to_right = jnp.concatenate([
                jnp.concatenate([own_l[n, a_of], own_l[n, b_of], far_r[n, b_of], far_r[n, a_of]], axis=1)
                for n in (c, c + 1)
            ], axis=0)
            a, b = dot(to_left, wl[half]), dot(to_right, wr[half])
            for n in range(2):
                rows_of = pl.ds((c + n) * ch + half * g, g)
                an, bn = a[n * g : n * g + g], b[n * g : n * g + g]
                out_v[rows_of, :128] = an[:, :128].astype(BF)
                out_v[rows_of, 128:256] = (an[:, 128:] + bn[:, :128]).astype(BF)
                out_v[rows_of, 256:] = bn[:, 128:].astype(BF)
    for copy in started:
        copy.wait_send()


def local(nx, ny, npos, latent):
    rows = latent.shape[0]
    g = rows // CHUNKS // 2
    block = pltpu.VMEM((CHUNKS, 3 * g, 128), BF)
    return pl.pallas_call(
        functools.partial(kernel, nx, ny, npos),
        out_shape=jax.ShapeDtypeStruct(latent.shape, BF),
        in_specs=[pl.BlockSpec(memory_space=pltpu.HBM)],
        out_specs=pl.BlockSpec(memory_space=pltpu.VMEM),
        scratch_shapes=[
            pltpu.VMEM((rows, WIDE), BF),
            block, block, block, block, block, block,
            pltpu.VMEM((PRE * 2 * g, WIDE), BF),
            pltpu.VMEM((PRE * 2 * g, WIDE), BF),
            pltpu.VMEM((2, WIDE, 256), BF),
            pltpu.VMEM((2, WIDE, 256), BF),
            pltpu.VMEM((2, WIDE, 256), BF),
            pltpu.VMEM((2, WIDE, 256), BF),
            pltpu.VMEM((2, 512, 256), BF),
            pltpu.VMEM((2, 512, 256), BF),
            pltpu.VMEM((2, 256, 256), F32),
            pltpu.VMEM((2, 2, SUM, 128), BF),
            pltpu.VMEM((2, 2, max(nx, ny) - 1, SUM, 128), BF),
            pltpu.VMEM((2, PACK, 128), BF),
            pltpu.VMEM((2, PACK, 128), BF),
            pltpu.VMEM((2, PACK, 128), BF),
            pltpu.SemaphoreType.DMA((CHUNKS,)),
            pltpu.SemaphoreType.DMA((2, 2, len(PIECES), max(nx, ny) - 1)),
            pltpu.SemaphoreType.DMA((2, 2, len(PIECES), max(nx, ny) - 1)),
            pltpu.SemaphoreType.DMA((4, CHUNKS)),
            pltpu.SemaphoreType.DMA((4, CHUNKS)),
            pltpu.SemaphoreType.DMA((2, 2)),
            pltpu.SemaphoreType.DMA((2, 2)),
            pltpu.SemaphoreType.DMA((2,)),
            pltpu.SemaphoreType.DMA((2,)),
        ],
        compiler_params=pltpu.CompilerParams(
            collective_id=0, has_side_effects=True, vmem_limit_bytes=54_000_000
        ),
    )(latent)


def solution(mesh):
    side = math.isqrt(mesh.shape["rows"])
    return jax.shard_map(
        functools.partial(local, side, mesh.shape["rows"] // side, mesh.shape["pairs"]),
        mesh=mesh,
        in_specs=(P("rows", "pairs"),),
        out_specs=P("rows", "pairs"),
        check_vma=False,
    )
```

```python
import functools
import math

import jax
import jax.numpy as jnp
from jax import lax
from jax.experimental import pallas as pl
from jax.experimental.pallas import tpu as pltpu
from jax.sharding import PartitionSpec as P

BF = jnp.bfloat16
F32 = jnp.float32
BLK = 192
WIDE = 2 * BLK
CHUNKS = 8
PRE = 4
PACK = 288
SUM = 304
PIECES = ((0, 0, 144), (1, 144, 160))
LOADS = 4
MESH = pl.DeviceIdType.MESH


def polynomial():
    a = 1.5 / math.sqrt(65.0)
    t = a * a
    f = [2.25, -2.4375, 1.6875, -0.5625, 0.0625]
    c = []
    for k in range(5):
        c.append(a * sum(f[n] * math.comb(n, k) * t ** (n - k) for n in range(k, 5)))
    return t, c


def dot(a, b):
    return jnp.dot(a, b, preferred_element_type=F32)


def dot_nt(a, b):
    return lax.dot_general(a, b, (((1,), (1,)), ((), ())), preferred_element_type=F32)


def dot_tn(a, b):
    return lax.dot_general(a, b, (((0,), (0,)), ((), ())), preferred_element_type=F32)


def iota(shape, dim):
    return lax.broadcasted_iota(jnp.int32, shape, dim)


def series(h, c, full, eye):
    hb = h.astype(BF)
    h2 = dot(hb, full(hb))
    rest = c[1] * h + c[2] * h2 + dot(h2.astype(BF), full((c[3] * h + c[4] * h2).astype(BF)))
    return jnp.where(eye, rest + c[0], rest), full(rest.astype(BF))


def below(x):
    return jnp.concatenate([x, jnp.zeros((64, 256), x.dtype)], axis=0)


def above(x):
    return jnp.concatenate([jnp.zeros((64, 256), x.dtype), x], axis=0)


def scale_of(corr):
    square = jnp.sum(jnp.sum(corr * corr, axis=0, keepdims=True), axis=1, keepdims=True)
    return 8.0 * lax.rsqrt(2.0 * square + 1e-12)


def left_columns(corr, scale):
    t, c = polynomial()
    cb = corr.astype(BF)
    row, lane = iota((BLK, 256), 0), iota((BLK, 256), 1)
    ct = below(corr).T[64:]
    q1, p1 = series((t * scale * scale) * dot_nt(cb, below(cb)), c, below, row == lane)
    return q1, -scale * (c[0] * ct + dot(ct.astype(BF), p1))


def right_columns(corr, scale):
    t, c = polynomial()
    cb = corr.astype(BF)
    ctb = below(corr).T[64:].astype(BF)
    row, lane = iota((BLK, 256), 0), iota((BLK, 256), 1)
    q2, p2 = series((t * scale * scale) * dot_nt(ctb, above(ctb)), c, above, row + 64 == lane)
    return scale * (c[0] * corr + dot(cb, p2)), q2


def rolled(x):
    return pltpu.roll(x, 64, axis=1)


def packed(x):
    lane = iota((BLK // 2, 128), 1)
    low, high = x[: BLK // 2, :128], x[BLK // 2 :, :128]
    return jnp.concatenate([x[:, 128:], jnp.where(lane >= 64, low, rolled(high))], axis=0)


def unpacked(x):
    lane = iota((BLK // 2, 128), 1)
    shared = x[BLK:PACK]
    low = jnp.where(lane >= 64, shared, 0.0)
    high = jnp.where(lane >= 64, rolled(shared), 0.0)
    return jnp.concatenate([jnp.concatenate([low, high], axis=0), x[:BLK]], axis=1)


def sent_sum(gram, left_sq, right_sq):
    row = iota((SUM - PACK, 128), 0)
    side = jnp.zeros((SUM - PACK, 128), F32)
    for n, value in enumerate((left_sq[:, :128], left_sq[:, 128:], right_sq[:, :128], right_sq[:, 128:])):
        side = jnp.where(row == n, value, side)
    return jnp.concatenate([packed(gram), side], axis=0).astype(BF)


def corr_of(total):
    gram, n = unpacked(total), total[PACK:]
    row, lane = iota((BLK, 128), 0), iota((BLK, 128), 1)
    left_sq = jnp.where(row < 128, n[0:1], n[1:2])
    left_sq = jnp.where(lane == lax.rem(row, 128), left_sq, 0.0)
    left_sq = jnp.sum(left_sq, axis=1, keepdims=True)
    right_sq = jnp.concatenate([n[2:3], n[3:4]], axis=1)
    corr = gram * lax.rsqrt(left_sq) * lax.rsqrt(right_sq)
    return jnp.where(iota((BLK, 256), 1) >= 64, corr, 0.0)


def keep_left(ref, q1, nkt):
    for rows_of, value in ((pl.ds(0, BLK), q1), (pl.ds(BLK, BLK), nkt)):
        ref[0, rows_of] = value.astype(BF)
        ref[1, rows_of, :128] = value[:, :128].astype(BF)
        ref[1, rows_of, 128:] = rolled(value[:, 128:]).astype(BF)


def keep_right(ref, k, q2):
    for rows_of, value in ((pl.ds(0, BLK), k), (pl.ds(BLK, BLK), q2)):
        ref[0, rows_of] = value.astype(BF)
        ref[1, rows_of, :128] = rolled(value[:, :128]).astype(BF)
        ref[1, rows_of, 128:] = value[:, 128:].astype(BF)


def kernel(
    nx, ny, npos,
    w_hbm, out_v,
    w, own_l, own_r, in_l, in_r, far_l, far_r, raw_l, raw_r,
    ql, qr, pql, nqr, wl, acc, part, got, c_own, c_prev, c_next,
    load_sem, sum_send, sum_recv, mv_send, in_recv, far_recv, c_send, c_recv, raw_send, raw_recv,
):
    r, p = lax.axis_index("rows"), lax.axis_index("pairs")
    x, y = lax.rem(r, nx), lax.div(r, nx)
    nxt, prv = lax.rem(p + 1, npos), lax.rem(p + npos - 1, npos)
    rows = w_hbm.shape[0]
    ch = rows // CHUNKS
    g = ch // 2

    def along(axis, k):
        if axis == 0:
            return (y * nx + lax.rem(x + k, nx), p)
        return (lax.rem(y + k, ny) * nx + x, p)

    ring = (nx, ny)
    peers = [along(a, k) for a in (0, 1) for k in range(1, ring[a])] + [(r, nxt), (r, prv)]

    piece = rows // LOADS
    loads = [
        pltpu.make_async_copy(
            w_hbm.at[pl.ds(c * piece, piece)], w.at[pl.ds(c * piece, piece)], load_sem.at[c]
        )
        for c in range(LOADS)
    ]
    for copy in loads:
        copy.start()
    barrier = pltpu.get_barrier_semaphore()
    for peer in peers:
        pl.semaphore_signal(barrier, inc=1, device_id=peer, device_id_type=MESH)

    def remote(src, dst, send, recv, target):
        pltpu.make_async_remote_copy(
            src_ref=src, dst_ref=dst, send_sem=send, recv_sem=recv,
            device_id=target, device_id_type=MESH,
        ).start()

    def arrived(ref, sem):
        pltpu.make_async_copy(ref, ref, sem).wait()

    def pieces_of(phase, n):
        first, start, size = PIECES[n]
        axis = (phase + first) % 2
        return axis, pl.ds(start, size), pl.ds(0, ring[axis] - 1)

    def send_piece(rnd, phase, n):
        axis, rows_of, _ = pieces_of(phase, n)
        for k in (2, 1, 3):
            if k < ring[axis]:
                remote(
                    part.at[rnd, phase, rows_of], got.at[rnd, phase, k - 1, rows_of],
                    sum_send.at[rnd, phase, n], sum_recv.at[rnd, phase, n], along(axis, k),
                )

    def collect(rnd, phase, n):
        axis, rows_of, slots = pieces_of(phase, n)
        arrived(got.at[rnd, phase, slots, rows_of], sum_recv.at[rnd, phase, n])
        total = part[rnd, phase, rows_of].astype(F32)
        for k in range(ring[axis] - 1):
            total = total + got[rnd, phase, k, rows_of].astype(F32)
        return total

    def start_sum(rnd, payload):
        part[rnd, 0] = payload
        for n in range(2):
            send_piece(rnd, 0, n)

    def end_sum(rnd):
        for n in range(2):
            part[rnd, 1, pl.ds(PIECES[n][1], PIECES[n][2])] = collect(rnd, 0, n).astype(BF)
            send_piece(rnd, 1, n)
        return jnp.concatenate([collect(rnd, 1, n) for n in range(2)], axis=0)

    def sum_sent(rnd):
        for phase in range(2):
            for n in range(2):
                _, rows_of, slots = pieces_of(phase, n)
                arrived(got.at[rnd, phase, slots, rows_of], sum_send.at[rnd, phase, n])

    def exchange(rnd, corr):
        c_own[rnd] = packed(corr).astype(BF)
        remote(c_own.at[rnd], c_prev.at[rnd], c_send.at[rnd], c_recv.at[rnd, 0], (r, nxt))
        remote(c_own.at[rnd], c_next.at[rnd], c_send.at[rnd], c_recv.at[rnd, 1], (r, prv))

    def turn_left(c, src, weights, dst):
        a = dot(src[pl.ds(c * ch, g)], weights[0])
        b = dot(src[pl.ds(c * ch + g, g)], weights[1])
        dst[c, :g] = a[:, :128].astype(BF)
        dst[c, g : 2 * g] = b[:, :128].astype(BF)
        dst[c, 2 * g :] = (a[:, 128:] + b[:, 128:]).astype(BF)

    def turn_right(c, src, weights, dst):
        a = dot(src[pl.ds(c * ch, g)], weights[0])
        b = dot(src[pl.ds(c * ch + g, g)], weights[1])
        dst[c, :g] = a[:, 128:].astype(BF)
        dst[c, g : 2 * g] = b[:, 128:].astype(BF)
        dst[c, 2 * g :] = (a[:, :128] + b[:, :128]).astype(BF)

    early = pl.ds(0, PRE * ch)
    for c in range(PRE * ch // piece):
        loads[c].wait()
    pl.semaphore_wait(barrier, len(peers))
    remote(w.at[early], raw_l, raw_send, raw_recv.at[0], (r, nxt))
    remote(w.at[early], raw_r, raw_send, raw_recv.at[1], (r, prv))

    sq = jnp.zeros((8, WIDE), F32)
    for c in range(LOADS):
        if c * piece >= PRE * ch:
            loads[c].wait()
        block = w[pl.ds(c * piece, piece)]
        new = dot_tn(block[:, :256], block[:, 128:])[:BLK]
        if c == 0:
            acc[...] = new
        else:
            acc[...] += new
        wide = block.astype(F32)
        sq = sq + jnp.sum((wide * wide).reshape(piece // 8, 8, WIDE), axis=0)
    sq = jnp.sum(sq, axis=0, keepdims=True)
    start_sum(0, sent_sum(acc[...], sq[:, :256], sq[:, 128:]))
    corr = corr_of(end_sum(0))
    exchange(0, corr)
    scale = scale_of(corr)
    keep_left(ql, *left_columns(corr, scale))
    keep_right(qr, *right_columns(corr, scale))

    for c in range(PRE, CHUNKS):
        turn_left(c, w, ql, own_l)
        remote(own_l.at[c], in_l.at[c], mv_send.at[0], in_recv.at[0, c - PRE], (r, nxt))
        turn_right(c, w, qr, own_r)
        remote(own_r.at[c], in_r.at[c], mv_send.at[1], in_recv.at[1, c - PRE], (r, prv))
    arrived(c_prev.at[0], c_recv.at[0, 0])
    arrived(c_next.at[0], c_recv.at[0, 1])
    corr = unpacked(c_prev[0].astype(F32))
    keep_left(pql, *left_columns(corr, scale_of(corr)))
    corr = unpacked(c_next[0].astype(F32))
    keep_right(nqr, *right_columns(corr, scale_of(corr)))

    sq_l = [jnp.zeros((8, 128), F32), jnp.zeros((8, 128), F32)]
    sq_r = [jnp.zeros((8, 128), F32), jnp.zeros((8, 128), F32)]

    def squares(total, block):
        wide = block.astype(F32)
        wide = wide * wide
        a = jnp.sum(wide[: 2 * g].reshape(2 * g // 8, 8, 128), axis=0)
        b = jnp.sum(wide[2 * g :].reshape(g // 8, 8, 128), axis=0)
        return [total[0] + a, total[1] + b]

    for c in range(CHUNKS):
        if c == 0:
            arrived(raw_l, raw_recv.at[0])
            arrived(raw_r, raw_recv.at[1])
        if c < PRE:
            turn_left(c, raw_l, pql, in_l)
            turn_right(c, raw_r, nqr, in_r)
        else:
            arrived(in_l.at[c], in_recv.at[0, c - PRE])
            arrived(in_r.at[c], in_recv.at[1, c - PRE])
        remote(in_l.at[c], far_l.at[c], mv_send.at[2], far_recv.at[0], (r, nxt))
        remote(in_r.at[c], far_r.at[c], mv_send.at[3], far_recv.at[1], (r, prv))
        left, right = in_l[c], in_r[c]
        lb, rb = left[2 * g :], right[2 * g :]
        a = jnp.concatenate([left[: 2 * g], jnp.concatenate([lb, rolled(lb)], axis=0)], axis=1)
        b = jnp.concatenate([jnp.concatenate([rb, rolled(rb)], axis=0), right[: 2 * g]], axis=1)
        new = dot_tn(a, b)[:BLK]
        if c == 0:
            acc[...] = new
        else:
            acc[...] += new
        sq_l = squares(sq_l, left)
        sq_r = squares(sq_r, right)

    def folded(total):
        a, b = (jnp.sum(v, axis=0, keepdims=True) for v in total)
        return a, b + rolled(b)

    la, lb = folded(sq_l)
    ra, rb = folded(sq_r)
    start_sum(1, sent_sum(
        acc[...], jnp.concatenate([la, lb], axis=1), jnp.concatenate([rb, ra], axis=1)
    ))
    for c in range(PRE):
        turn_left(c, w, ql, own_l)
        turn_right(c, w, qr, own_r)
    sum_sent(0)
    for side in range(2):
        arrived((own_l, own_r)[side].at[pl.ds(PRE, CHUNKS - PRE)], mv_send.at[side])
    arrived(w.at[pl.ds(0, 2 * PRE * ch)], raw_send)
    arrived(c_prev, c_send.at[0])
    exchange(1, corr_of(end_sum(1)))

    none = jnp.zeros((64, 256), BF)

    def keep_last(ref, top, low):
        top, low = top.astype(BF), low.astype(BF)
        ref[0, :BLK] = top
        ref[0, BLK:256] = none
        ref[1, :128] = top[:128]
        ref[1, 128:192] = none
        ref[1, 192:256] = top[128:]
        ref[0, 256:320] = none
        ref[0, 320:] = low
        ref[1, 256:320] = low[:64]
        ref[1, 320:384] = none
        ref[1, 384:] = low[64:]

    def finish(side, first):
        from_l, from_r = ((far_l, own_r), (own_l, far_r))[side]
        arrived((c_prev, c_next)[side].at[1], c_recv.at[1, side])
        corr = unpacked((c_prev, c_next)[side][1].astype(F32))
        keep_last(wl, *(left_columns, right_columns)[side](corr, scale_of(corr)))
        arrived((far_l, far_r)[side], far_recv.at[side])
        outer = (pl.ds(0, 128), pl.ds(256, 128))[side]
        for c in range(0, CHUNKS, 4):
            for half in range(2):
                a_of, b_of = pl.ds(half * g, g), pl.ds(2 * g, g)
                terms = jnp.concatenate([
                    jnp.concatenate(
                        [from_l[n, a_of], from_l[n, b_of], from_r[n, b_of], from_r[n, a_of]], axis=1
                    )
                    for n in range(c, c + 4)
                ], axis=0)
                a = dot(terms, wl[half])
                for n in range(4):
                    rows_of = pl.ds((c + n) * ch + half * g, g)
                    pair = a[n * g : n * g + g, :128], a[n * g : n * g + g, 128:]
                    out_v[rows_of, outer] = pair[side].astype(BF)
                    middle = pair[1 - side]
                    if not first:
                        middle = middle + out_v[rows_of, 128:256].astype(F32)
                    out_v[rows_of, 128:256] = middle.astype(BF)

    @pl.when(lax.rem(p, 2) == 0)
    def _():
        finish(1, True)
        finish(0, False)

    @pl.when(lax.rem(p, 2) == 1)
    def _():
        finish(0, True)
        finish(1, False)

    sum_sent(1)
    arrived(in_l, mv_send.at[2])
    arrived(in_r, mv_send.at[3])
    arrived(c_prev, c_send.at[1])


def local(nx, ny, npos, latent):
    rows = latent.shape[0]
    g = rows // CHUNKS // 2
    block = pltpu.VMEM((CHUNKS, 3 * g, 128), BF)
    return pl.pallas_call(
        functools.partial(kernel, nx, ny, npos),
        out_shape=jax.ShapeDtypeStruct(latent.shape, BF),
        in_specs=[pl.BlockSpec(memory_space=pltpu.HBM)],
        out_specs=pl.BlockSpec(memory_space=pltpu.VMEM),
        scratch_shapes=[
            pltpu.VMEM((rows, WIDE), BF),
            block, block, block, block, block, block,
            pltpu.VMEM((PRE * 2 * g, WIDE), BF),
            pltpu.VMEM((PRE * 2 * g, WIDE), BF),
            pltpu.VMEM((2, WIDE, 256), BF),
            pltpu.VMEM((2, WIDE, 256), BF),
            pltpu.VMEM((2, WIDE, 256), BF),
            pltpu.VMEM((2, WIDE, 256), BF),
            pltpu.VMEM((2, 512, 256), BF),
            pltpu.VMEM((BLK, 256), F32),
            pltpu.VMEM((2, 2, SUM, 128), BF),
            pltpu.VMEM((2, 2, max(nx, ny) - 1, SUM, 128), BF),
            pltpu.VMEM((2, PACK, 128), BF),
            pltpu.VMEM((2, PACK, 128), BF),
            pltpu.VMEM((2, PACK, 128), BF),
            pltpu.SemaphoreType.DMA((LOADS,)),
            pltpu.SemaphoreType.DMA((2, 2, len(PIECES))),
            pltpu.SemaphoreType.DMA((2, 2, len(PIECES))),
            pltpu.SemaphoreType.DMA((4,)),
            pltpu.SemaphoreType.DMA((2, CHUNKS - PRE)),
            pltpu.SemaphoreType.DMA((2,)),
            pltpu.SemaphoreType.DMA((2,)),
            pltpu.SemaphoreType.DMA((2, 2)),
            pltpu.SemaphoreType.DMA,
            pltpu.SemaphoreType.DMA((2,)),
        ],
        compiler_params=pltpu.CompilerParams(
            collective_id=0, has_side_effects=True, vmem_limit_bytes=54_000_000
        ),
    )(latent)


def solution(mesh):
    side = math.isqrt(mesh.shape["rows"])
    return jax.shard_map(
        functools.partial(local, side, mesh.shape["rows"] // side, mesh.shape["pairs"]),
        mesh=mesh,
        in_specs=(P("rows", "pairs"),),
        out_specs=P("rows", "pairs"),
        check_vma=False,
    )
```

```python
import functools
import math

import jax
import jax.numpy as jnp
from jax import lax
from jax.experimental import pallas as pl
from jax.experimental.pallas import tpu as pltpu
from jax.sharding import PartitionSpec as P

BF = jnp.bfloat16
F32 = jnp.float32
BLK = 192
WIDE = 2 * BLK
CHUNKS = 8
PRE = 4
PACK = 288
SUM = 304
PIECES = ((0, 0, 144), (1, 144, 160))
LOADS = 4
TILE = 16
LATE = 2
MESH = pl.DeviceIdType.MESH


def polynomial():
    a = 1.5 / math.sqrt(65.0)
    t = a * a
    f = [2.25, -2.4375, 1.6875, -0.5625, 0.0625]
    c = []
    for k in range(5):
        c.append(a * sum(f[n] * math.comb(n, k) * t ** (n - k) for n in range(k, 5)))
    return t, c


def dot(a, b):
    return jnp.dot(a, b, preferred_element_type=F32)


def dot_nt(a, b):
    return lax.dot_general(a, b, (((1,), (1,)), ((), ())), preferred_element_type=F32)


def dot_tn(a, b):
    return lax.dot_general(a, b, (((0,), (0,)), ((), ())), preferred_element_type=F32)


def iota(shape, dim):
    return lax.broadcasted_iota(jnp.int32, shape, dim)


def series(h, c, full, eye):
    hb = h.astype(BF)
    h2 = dot(hb, full(hb))
    rest = c[1] * h + c[2] * h2 + dot(h2.astype(BF), full((c[3] * h + c[4] * h2).astype(BF)))
    return jnp.where(eye, rest + c[0], rest), full(rest.astype(BF))


def below(x):
    return jnp.concatenate([x, jnp.zeros((64, 256), x.dtype)], axis=0)


def above(x):
    return jnp.concatenate([jnp.zeros((64, 256), x.dtype), x], axis=0)


def scale_of(corr):
    square = jnp.sum(jnp.sum(corr * corr, axis=0, keepdims=True), axis=1, keepdims=True)
    return 8.0 * lax.rsqrt(2.0 * square + 1e-12)


def left_columns(corr, scale):
    t, c = polynomial()
    cb = corr.astype(BF)
    row, lane = iota((BLK, 256), 0), iota((BLK, 256), 1)
    ct = below(corr).T[64:]
    q1, p1 = series((t * scale * scale) * dot_nt(cb, below(cb)), c, below, row == lane)
    return q1, -scale * (c[0] * ct + dot(ct.astype(BF), p1))


def right_columns(corr, scale):
    t, c = polynomial()
    cb = corr.astype(BF)
    ctb = below(corr).T[64:].astype(BF)
    row, lane = iota((BLK, 256), 0), iota((BLK, 256), 1)
    q2, p2 = series((t * scale * scale) * dot_nt(ctb, above(ctb)), c, above, row + 64 == lane)
    return scale * (c[0] * corr + dot(cb, p2)), q2


def rolled(x):
    return pltpu.roll(x, 64, axis=1)


def packed(x):
    lane = iota((BLK // 2, 128), 1)
    low, high = x[: BLK // 2, :128], x[BLK // 2 :, :128]
    return jnp.concatenate([x[:, 128:], jnp.where(lane >= 64, low, rolled(high))], axis=0)


def unpacked(x):
    lane = iota((BLK // 2, 128), 1)
    shared = x[BLK:PACK]
    low = jnp.where(lane >= 64, shared, 0.0)
    high = jnp.where(lane >= 64, rolled(shared), 0.0)
    return jnp.concatenate([jnp.concatenate([low, high], axis=0), x[:BLK]], axis=1)


def sent_sum(gram, left_sq, right_sq):
    row = iota((SUM - PACK, 128), 0)
    side = jnp.zeros((SUM - PACK, 128), F32)
    for n, value in enumerate((left_sq[:, :128], left_sq[:, 128:], right_sq[:, :128], right_sq[:, 128:])):
        side = jnp.where(row == n, value, side)
    return jnp.concatenate([packed(gram), side], axis=0).astype(BF)


def corr_of(total):
    gram, n = unpacked(total), total[PACK:]
    row, lane = iota((BLK, 128), 0), iota((BLK, 128), 1)
    left_sq = jnp.where(row < 128, n[0:1], n[1:2])
    left_sq = jnp.where(lane == lax.rem(row, 128), left_sq, 0.0)
    left_sq = jnp.sum(left_sq, axis=1, keepdims=True)
    right_sq = jnp.concatenate([n[2:3], n[3:4]], axis=1)
    corr = gram * lax.rsqrt(left_sq) * lax.rsqrt(right_sq)
    return jnp.where(iota((BLK, 256), 1) >= 64, corr, 0.0)


def keep_left(ref, q1, nkt):
    for rows_of, value in ((pl.ds(0, BLK), q1), (pl.ds(BLK, BLK), nkt)):
        ref[0, rows_of] = value.astype(BF)
        ref[1, rows_of, :128] = value[:, :128].astype(BF)
        ref[1, rows_of, 128:] = rolled(value[:, 128:]).astype(BF)


def keep_right(ref, k, q2):
    for rows_of, value in ((pl.ds(0, BLK), k), (pl.ds(BLK, BLK), q2)):
        ref[0, rows_of] = value.astype(BF)
        ref[1, rows_of, :128] = rolled(value[:, :128]).astype(BF)
        ref[1, rows_of, 128:] = value[:, 128:].astype(BF)


def kernel(
    nx, ny, npos,
    w_hbm, out_v,
    w, own_l, own_r, in_l, in_r, far_l, far_r, raw_l, raw_r,
    ql, qr, pql, nqr, wl, acc, part, got, c_own, c_both,
    tile_got, rest_got, sums, tot_prev, tot_next,
    load_sem, sum_send, sum_recv, mv_send, in_recv, far_recv, c_send, c_recv, raw_send, raw_recv,
    tile_send, tile_recv, rest_send, rest_recv, spread_send, tot_recv,
):
    r, p = lax.axis_index("rows"), lax.axis_index("pairs")
    x, y = lax.rem(r, nx), lax.div(r, nx)
    nxt, prv = lax.rem(p + 1, npos), lax.rem(p + npos - 1, npos)
    rows = w_hbm.shape[0]
    ch = rows // CHUNKS
    g = ch // 2

    def along(axis, k):
        if axis == 0:
            return (y * nx + lax.rem(x + k, nx), p)
        return (lax.rem(y + k, ny) * nx + x, p)

    ring = (nx, ny)
    c_prev, c_next = c_both.at[0], c_both.at[1]
    peers = [along(a, k) for a in (0, 1) for k in range(1, ring[a])] + [(r, nxt), (r, prv)]

    piece = rows // LOADS
    loads = [
        pltpu.make_async_copy(
            w_hbm.at[pl.ds(c * piece, piece)], w.at[pl.ds(c * piece, piece)], load_sem.at[c]
        )
        for c in range(LOADS)
    ]
    for copy in loads:
        copy.start()
    barrier = pltpu.get_barrier_semaphore()
    for peer in peers:
        pl.semaphore_signal(barrier, inc=1, device_id=peer, device_id_type=MESH)

    def remote(src, dst, send, recv, target):
        pltpu.make_async_remote_copy(
            src_ref=src, dst_ref=dst, send_sem=send, recv_sem=recv,
            device_id=target, device_id_type=MESH,
        ).start()

    def arrived(ref, sem):
        pltpu.make_async_copy(ref, ref, sem).wait()

    def pieces_of(phase, n):
        first, start, size = PIECES[n]
        axis = (phase + first) % 2
        return axis, pl.ds(start, size), pl.ds(0, ring[axis] - 1)

    def send_piece(phase, n):
        axis, rows_of, _ = pieces_of(phase, n)
        for k in (2, 1, 3):
            if k < ring[axis]:
                remote(
                    part.at[0, phase, rows_of], got.at[phase, k - 1, rows_of],
                    sum_send.at[phase, n], sum_recv.at[phase, n], along(axis, k),
                )

    def collect(phase, n):
        axis, rows_of, slots = pieces_of(phase, n)
        arrived(got.at[phase, slots, rows_of], sum_recv.at[phase, n])
        total = part[0, phase, rows_of].astype(F32)
        for k in range(ring[axis] - 1):
            total = total + got[phase, k, rows_of].astype(F32)
        return total

    def start_sum(payload):
        part[0, 0] = payload
        for n in range(2):
            send_piece(0, n)

    def end_sum():
        for n in range(2):
            part[0, 1, pl.ds(PIECES[n][1], PIECES[n][2])] = collect(0, n).astype(BF)
            send_piece(1, n)
        return jnp.concatenate([collect(1, n) for n in range(2)], axis=0)

    def sum_sent():
        for phase in range(2):
            for n in range(2):
                _, rows_of, slots = pieces_of(phase, n)
                arrived(got.at[phase, slots, rows_of], sum_send.at[phase, n])

    def exchange(corr):
        c_own[...] = packed(corr).astype(BF)
        remote(c_own, c_prev, c_send, c_recv.at[0], (r, nxt))
        remote(c_own, c_next, c_send, c_recv.at[1], (r, prv))

    plane = nx * ny
    slots, rest = divmod(SUM // TILE, plane)
    final = part.at[1, 0]
    peer_at = [lax.rem(r + k, plane) for k in range(plane)]

    def tile(n):
        return pl.ds(n * TILE if isinstance(n, int) else pl.multiple_of(n * TILE, TILE), TILE)

    def scatter(payload):
        part[1, 0] = payload
        for j in range(rest):
            n = slots * plane + j

            @pl.when(r != j)
            def _():
                remote(
                    final.at[tile(n)], rest_got.at[lax.rem(r - j + plane, plane) - 1],
                    rest_send.at[j], rest_recv, (j, p),
                )

        for s in range(slots):
            for k in range(1, plane):
                remote(
                    final.at[tile(s * plane + peer_at[k])], tile_got.at[s, k - 1],
                    tile_send, tile_recv, (peer_at[k], p),
                )

    def gather():
        def spread(src, n, send):
            for k in range(plane):
                remote(src, tot_prev.at[tile(n)], send.at[0], tot_recv.at[0], (peer_at[k], nxt))
                remote(src, tot_next.at[tile(n)], send.at[1], tot_recv.at[1], (peer_at[k], prv))

        arrived(tile_got, tile_recv)
        for s in range(slots):
            n = s * plane + r
            total = part[1, 0, tile(n)].astype(F32)
            for k in range(plane - 1):
                total = total + tile_got[s, k].astype(F32)
            sums[s] = total.astype(BF)
            spread(sums.at[s], n, spread_send.at[s])

        @pl.when(r < rest)
        def _():
            n = slots * plane + r
            arrived(rest_got, rest_recv)
            total = part[1, 0, tile(n)].astype(F32)
            for k in range(plane - 1):
                total = total + rest_got[k].astype(F32)
            sums[slots] = total.astype(BF)
            spread(sums.at[slots], n, spread_send.at[slots])

    def gathered():
        everyone = pl.ds(0, plane * TILE)
        for j in range(rest):
            @pl.when(r != j)
            def _():
                arrived(final.at[tile(slots * plane + j)], rest_send.at[j])
        arrived(tile_got, tile_send)
        for s in range(slots):
            for side in range(2):
                arrived(tot_prev.at[everyone], spread_send.at[s, side])

        @pl.when(r < rest)
        def _():
            for side in range(2):
                arrived(tot_prev.at[everyone], spread_send.at[slots, side])

    def forward(c):
        remote(in_l.at[c], far_l.at[c], mv_send.at[2], far_recv.at[0], (r, nxt))
        remote(in_r.at[c], far_r.at[c], mv_send.at[3], far_recv.at[1], (r, prv))

    def turn_left(c, src, weights, dst):
        a = dot(src[pl.ds(c * ch, g)], weights[0])
        b = dot(src[pl.ds(c * ch + g, g)], weights[1])
        dst[c, :g] = a[:, :128].astype(BF)
        dst[c, g : 2 * g] = b[:, :128].astype(BF)
        dst[c, 2 * g :] = (a[:, 128:] + b[:, 128:]).astype(BF)

    def turn_right(c, src, weights, dst):
        a = dot(src[pl.ds(c * ch, g)], weights[0])
        b = dot(src[pl.ds(c * ch + g, g)], weights[1])
        dst[c, :g] = a[:, 128:].astype(BF)
        dst[c, g : 2 * g] = b[:, 128:].astype(BF)
        dst[c, 2 * g :] = (a[:, :128] + b[:, :128]).astype(BF)

    early = pl.ds(0, PRE * ch)
    for c in range(PRE * ch // piece):
        loads[c].wait()
    pl.semaphore_wait(barrier, len(peers))
    remote(w.at[early], raw_l, raw_send, raw_recv.at[0], (r, nxt))
    remote(w.at[early], raw_r, raw_send, raw_recv.at[1], (r, prv))

    sq = jnp.zeros((8, WIDE), F32)
    for c in range(LOADS):
        if c * piece >= PRE * ch:
            loads[c].wait()
        block = w[pl.ds(c * piece, piece)]
        new = dot_tn(block[:, :256], block[:, 128:])[:BLK]
        if c == 0:
            acc[...] = new
        else:
            acc[...] += new
        wide = block.astype(F32)
        sq = sq + jnp.sum((wide * wide).reshape(piece // 8, 8, WIDE), axis=0)
    sq = jnp.sum(sq, axis=0, keepdims=True)
    start_sum(sent_sum(acc[...], sq[:, :256], sq[:, 128:]))
    corr = corr_of(end_sum())
    exchange(corr)
    scale = scale_of(corr)
    keep_left(ql, *left_columns(corr, scale))
    keep_right(qr, *right_columns(corr, scale))

    for c in range(PRE, CHUNKS):
        turn_left(c, w, ql, own_l)
        remote(own_l.at[c], in_l.at[c], mv_send.at[0], in_recv.at[0, c - PRE], (r, nxt))
        turn_right(c, w, qr, own_r)
        remote(own_r.at[c], in_r.at[c], mv_send.at[1], in_recv.at[1, c - PRE], (r, prv))
    arrived(c_prev, c_recv.at[0])
    arrived(c_next, c_recv.at[1])
    corr = unpacked(c_prev[...].astype(F32))
    keep_left(pql, *left_columns(corr, scale_of(corr)))
    corr = unpacked(c_next[...].astype(F32))
    keep_right(nqr, *right_columns(corr, scale_of(corr)))

    sq_l = [jnp.zeros((8, 128), F32), jnp.zeros((8, 128), F32)]
    sq_r = [jnp.zeros((8, 128), F32), jnp.zeros((8, 128), F32)]

    def squares(total, block):
        wide = block.astype(F32)
        wide = wide * wide
        a = jnp.sum(wide[: 2 * g].reshape(2 * g // 8, 8, 128), axis=0)
        b = jnp.sum(wide[2 * g :].reshape(g // 8, 8, 128), axis=0)
        return [total[0] + a, total[1] + b]

    for c in range(CHUNKS):
        if c == 0:
            arrived(raw_l, raw_recv.at[0])
            arrived(raw_r, raw_recv.at[1])
        if c < PRE:
            turn_left(c, raw_l, pql, in_l)
            turn_right(c, raw_r, nqr, in_r)
        else:
            arrived(in_l.at[c], in_recv.at[0, c - PRE])
            arrived(in_r.at[c], in_recv.at[1, c - PRE])
        if c < CHUNKS - LATE:
            forward(c)
        left, right = in_l[c], in_r[c]
        lb, rb = left[2 * g :], right[2 * g :]
        a = jnp.concatenate([left[: 2 * g], jnp.concatenate([lb, rolled(lb)], axis=0)], axis=1)
        b = jnp.concatenate([jnp.concatenate([rb, rolled(rb)], axis=0), right[: 2 * g]], axis=1)
        new = dot_tn(a, b)[:BLK]
        if c == 0:
            acc[...] = new
        else:
            acc[...] += new
        sq_l = squares(sq_l, left)
        sq_r = squares(sq_r, right)

    def folded(total):
        a, b = (jnp.sum(v, axis=0, keepdims=True) for v in total)
        return a, b + rolled(b)

    la, lb = folded(sq_l)
    ra, rb = folded(sq_r)
    scatter(sent_sum(
        acc[...], jnp.concatenate([la, lb], axis=1), jnp.concatenate([rb, ra], axis=1)
    ))
    for c in range(PRE):
        turn_left(c, w, ql, own_l)
        turn_right(c, w, qr, own_r)
    gather()
    for c in range(CHUNKS - LATE, CHUNKS):
        forward(c)
    sum_sent()
    for side in range(2):
        arrived((own_l, own_r)[side].at[pl.ds(PRE, CHUNKS - PRE)], mv_send.at[side])
    arrived(w.at[pl.ds(0, 2 * PRE * ch)], raw_send)
    arrived(c_both, c_send)

    none = jnp.zeros((64, 256), BF)

    def keep_last(ref, top, low):
        top, low = top.astype(BF), low.astype(BF)
        ref[0, :BLK] = top
        ref[0, BLK:256] = none
        ref[1, :128] = top[:128]
        ref[1, 128:192] = none
        ref[1, 192:256] = top[128:]
        ref[0, 256:320] = none
        ref[0, 320:] = low
        ref[1, 256:320] = low[:64]
        ref[1, 320:384] = none
        ref[1, 384:] = low[64:]

    def finish(side, first):
        from_l, from_r = ((far_l, own_r), (own_l, far_r))[side]
        total = (tot_prev, tot_next)[side]
        arrived(total, tot_recv.at[side])
        corr = corr_of(total[...].astype(F32))
        keep_last(wl, *(left_columns, right_columns)[side](corr, scale_of(corr)))
        arrived((far_l, far_r)[side], far_recv.at[side])
        outer = (pl.ds(0, 128), pl.ds(256, 128))[side]
        for c in range(0, CHUNKS, 4):
            for half in range(2):
                a_of, b_of = pl.ds(half * g, g), pl.ds(2 * g, g)
                terms = jnp.concatenate([
                    jnp.concatenate(
                        [from_l[n, a_of], from_l[n, b_of], from_r[n, b_of], from_r[n, a_of]], axis=1
                    )
                    for n in range(c, c + 4)
                ], axis=0)
                a = dot(terms, wl[half])
                for n in range(4):
                    rows_of = pl.ds((c + n) * ch + half * g, g)
                    pair = a[n * g : n * g + g, :128], a[n * g : n * g + g, 128:]
                    out_v[rows_of, outer] = pair[side].astype(BF)
                    middle = pair[1 - side]
                    if not first:
                        middle = middle + out_v[rows_of, 128:256].astype(F32)
                    out_v[rows_of, 128:256] = middle.astype(BF)

    @pl.when(lax.rem(p, 2) == 0)
    def _():
        finish(1, True)
        finish(0, False)

    @pl.when(lax.rem(p, 2) == 1)
    def _():
        finish(0, True)
        finish(1, False)

    gathered()
    arrived(in_l, mv_send.at[2])
    arrived(in_r, mv_send.at[3])


def local(nx, ny, npos, latent):
    rows = latent.shape[0]
    g = rows // CHUNKS // 2
    plane = nx * ny
    slots, rest = divmod(SUM // TILE, plane)
    block = pltpu.VMEM((CHUNKS, 3 * g, 128), BF)
    return pl.pallas_call(
        functools.partial(kernel, nx, ny, npos),
        out_shape=jax.ShapeDtypeStruct(latent.shape, BF),
        in_specs=[pl.BlockSpec(memory_space=pltpu.HBM)],
        out_specs=pl.BlockSpec(memory_space=pltpu.VMEM),
        scratch_shapes=[
            pltpu.VMEM((rows, WIDE), BF),
            block, block, block, block, block, block,
            pltpu.VMEM((PRE * 2 * g, WIDE), BF),
            pltpu.VMEM((PRE * 2 * g, WIDE), BF),
            pltpu.VMEM((2, WIDE, 256), BF),
            pltpu.VMEM((2, WIDE, 256), BF),
            pltpu.VMEM((2, WIDE, 256), BF),
            pltpu.VMEM((2, WIDE, 256), BF),
            pltpu.VMEM((2, 512, 256), BF),
            pltpu.VMEM((BLK, 256), F32),
            pltpu.VMEM((2, 2, SUM, 128), BF),
            pltpu.VMEM((2, max(nx, ny) - 1, SUM, 128), BF),
            pltpu.VMEM((PACK, 128), BF),
            pltpu.VMEM((2, PACK, 128), BF),
            pltpu.VMEM((slots, plane - 1, TILE, 128), BF),
            pltpu.VMEM((plane - 1, TILE, 128), BF),
            pltpu.VMEM((slots + 1, TILE, 128), BF),
            pltpu.VMEM((SUM, 128), BF),
            pltpu.VMEM((SUM, 128), BF),
            pltpu.SemaphoreType.DMA((LOADS,)),
            pltpu.SemaphoreType.DMA((2, len(PIECES))),
            pltpu.SemaphoreType.DMA((2, len(PIECES))),
            pltpu.SemaphoreType.DMA((4,)),
            pltpu.SemaphoreType.DMA((2, CHUNKS - PRE)),
            pltpu.SemaphoreType.DMA((2,)),
            pltpu.SemaphoreType.DMA,
            pltpu.SemaphoreType.DMA((2,)),
            pltpu.SemaphoreType.DMA,
            pltpu.SemaphoreType.DMA((2,)),
            pltpu.SemaphoreType.DMA,
            pltpu.SemaphoreType.DMA,
            pltpu.SemaphoreType.DMA((max(rest, 1),)),
            pltpu.SemaphoreType.DMA,
            pltpu.SemaphoreType.DMA((slots + 1, 2)),
            pltpu.SemaphoreType.DMA((2,)),
        ],
        compiler_params=pltpu.CompilerParams(
            collective_id=0, has_side_effects=True, vmem_limit_bytes=54_000_000
        ),
    )(latent)


def solution(mesh):
    side = math.isqrt(mesh.shape["rows"])
    return jax.shard_map(
        functools.partial(local, side, mesh.shape["rows"] // side, mesh.shape["pairs"]),
        mesh=mesh,
        in_specs=(P("rows", "pairs"),),
        out_specs=P("rows", "pairs"),
        check_vma=False,
    )
```

```python
import functools
import math

import jax
import jax.numpy as jnp
from jax import lax
from jax.experimental import pallas as pl
from jax.experimental.pallas import tpu as pltpu
from jax.sharding import PartitionSpec as P

BF = jnp.bfloat16
F32 = jnp.float32
BLK = 192
WIDE = 2 * BLK
CHUNKS = 8
PRE = 4
PACK = 288
SUM = 320
PIECES = ((0, 0, 144), (1, 144, 160))
LOADS = 4
TILE = 32
LATE = 2
MESH = pl.DeviceIdType.MESH


def polynomial():
    a = 1.5 / math.sqrt(65.0)
    t = a * a
    f = [2.25, -2.4375, 1.6875, -0.5625, 0.0625]
    c = []
    for k in range(5):
        c.append(a * sum(f[n] * math.comb(n, k) * t ** (n - k) for n in range(k, 5)))
    return t, c


def dot(a, b):
    return jnp.dot(a, b, preferred_element_type=F32)


def dot_nt(a, b):
    return lax.dot_general(a, b, (((1,), (1,)), ((), ())), preferred_element_type=F32)


def dot_tn(a, b):
    return lax.dot_general(a, b, (((0,), (0,)), ((), ())), preferred_element_type=F32)


def iota(shape, dim):
    return lax.broadcasted_iota(jnp.int32, shape, dim)


def series(h, c, full, eye):
    hb = h.astype(BF)
    h2 = dot(hb, full(hb))
    rest = c[1] * h + c[2] * h2 + dot(h2.astype(BF), full((c[3] * h + c[4] * h2).astype(BF)))
    return jnp.where(eye, rest + c[0], rest), full(rest.astype(BF))


def below(x):
    return jnp.concatenate([x, jnp.zeros((64, 256), x.dtype)], axis=0)


def above(x):
    return jnp.concatenate([jnp.zeros((64, 256), x.dtype), x], axis=0)


def scale_of(corr):
    square = jnp.sum(jnp.sum(corr * corr, axis=0, keepdims=True), axis=1, keepdims=True)
    return 8.0 * lax.rsqrt(2.0 * square + 1e-12)


def left_columns(corr, scale):
    t, c = polynomial()
    cb = corr.astype(BF)
    row, lane = iota((BLK, 256), 0), iota((BLK, 256), 1)
    ct = below(corr).T[64:]
    q1, p1 = series((t * scale * scale) * dot_nt(cb, below(cb)), c, below, row == lane)
    return q1, -scale * (c[0] * ct + dot(ct.astype(BF), p1))


def right_columns(corr, scale):
    t, c = polynomial()
    cb = corr.astype(BF)
    ctb = below(corr).T[64:].astype(BF)
    row, lane = iota((BLK, 256), 0), iota((BLK, 256), 1)
    q2, p2 = series((t * scale * scale) * dot_nt(ctb, above(ctb)), c, above, row + 64 == lane)
    return scale * (c[0] * corr + dot(cb, p2)), q2


def rolled(x):
    return pltpu.roll(x, 64, axis=1)


def packed(x):
    lane = iota((BLK // 2, 128), 1)
    low, high = x[: BLK // 2, :128], x[BLK // 2 :, :128]
    return jnp.concatenate([x[:, 128:], jnp.where(lane >= 64, low, rolled(high))], axis=0)


def unpacked(x):
    lane = iota((BLK // 2, 128), 1)
    shared = x[BLK:PACK]
    low = jnp.where(lane >= 64, shared, 0.0)
    high = jnp.where(lane >= 64, rolled(shared), 0.0)
    return jnp.concatenate([jnp.concatenate([low, high], axis=0), x[:BLK]], axis=1)


def sent_sum(gram, left_sq, right_sq):
    row = iota((SUM - PACK, 128), 0)
    side = jnp.zeros((SUM - PACK, 128), F32)
    for n, value in enumerate((left_sq[:, :128], left_sq[:, 128:], right_sq[:, :128], right_sq[:, 128:])):
        side = jnp.where(row == n, value, side)
    return jnp.concatenate([packed(gram), side], axis=0).astype(BF)


def corr_of(total):
    gram, n = unpacked(total), total[PACK:]
    row, lane = iota((BLK, 128), 0), iota((BLK, 128), 1)
    left_sq = jnp.where(row < 128, n[0:1], n[1:2])
    left_sq = jnp.where(lane == lax.rem(row, 128), left_sq, 0.0)
    left_sq = jnp.sum(left_sq, axis=1, keepdims=True)
    right_sq = jnp.concatenate([n[2:3], n[3:4]], axis=1)
    corr = gram * lax.rsqrt(left_sq) * lax.rsqrt(right_sq)
    return jnp.where(iota((BLK, 256), 1) >= 64, corr, 0.0)


def keep_left(ref, q1, nkt):
    for rows_of, value in ((pl.ds(0, BLK), q1), (pl.ds(BLK, BLK), nkt)):
        ref[0, rows_of] = value.astype(BF)
        ref[1, rows_of, :128] = value[:, :128].astype(BF)
        ref[1, rows_of, 128:] = rolled(value[:, 128:]).astype(BF)


def keep_right(ref, k, q2):
    for rows_of, value in ((pl.ds(0, BLK), k), (pl.ds(BLK, BLK), q2)):
        ref[0, rows_of] = value.astype(BF)
        ref[1, rows_of, :128] = rolled(value[:, :128]).astype(BF)
        ref[1, rows_of, 128:] = value[:, 128:].astype(BF)


def kernel(
    nx, ny, npos,
    w_hbm, out_v,
    w, own_l, own_r, in_l, in_r, far_l, far_r, raw,
    ql, qr, pql, nqr, wl, acc, part, got, c_own, c_both,
    tile_got, rest_got, sums, everyone, tot_prev, tot_next,
    load_sem, sum_send, sum_recv, mv_send, in_recv, far_recv, c_send, c_recv, raw_send, raw_recv,
    tile_send, tile_recv, rest_send, rest_recv, spread_send, tot_recv,
):
    r, p = lax.axis_index("rows"), lax.axis_index("pairs")
    x, y = lax.rem(r, nx), lax.div(r, nx)
    nxt, prv = lax.rem(p + 1, npos), lax.rem(p + npos - 1, npos)
    rows = w_hbm.shape[0]
    ch = rows // CHUNKS
    g = ch // 2

    def along(axis, k):
        if axis == 0:
            return (y * nx + lax.rem(x + k, nx), p)
        return (lax.rem(y + k, ny) * nx + x, p)

    ring = (nx, ny)
    raw_l, raw_r = raw.at[0], raw.at[1]
    c_prev, c_next = c_both.at[0], c_both.at[1]
    peers = [along(a, k) for a in (0, 1) for k in range(1, ring[a])] + [(r, nxt), (r, prv)]

    piece = rows // LOADS
    loads = [
        pltpu.make_async_copy(
            w_hbm.at[pl.ds(c * piece, piece)], w.at[pl.ds(c * piece, piece)], load_sem.at[c]
        )
        for c in range(LOADS)
    ]
    for copy in loads:
        copy.start()
    barrier = pltpu.get_barrier_semaphore()
    for peer in peers:
        pl.semaphore_signal(barrier, inc=1, device_id=peer, device_id_type=MESH)

    def remote(src, dst, send, recv, target):
        pltpu.make_async_remote_copy(
            src_ref=src, dst_ref=dst, send_sem=send, recv_sem=recv,
            device_id=target, device_id_type=MESH,
        ).start()

    def arrived(ref, sem):
        pltpu.make_async_copy(ref, ref, sem).wait()

    def pieces_of(phase, n):
        first, start, size = PIECES[n]
        axis = (phase + first) % 2
        return axis, pl.ds(start, size), pl.ds(0, ring[axis] - 1)

    def send_piece(phase, n):
        axis, rows_of, _ = pieces_of(phase, n)
        for k in (2, 1, 3):
            if k < ring[axis]:
                remote(
                    part.at[0, phase, rows_of], got.at[phase, k - 1, rows_of],
                    sum_send.at[phase, n], sum_recv.at[phase, n], along(axis, k),
                )

    def collect(phase, n):
        axis, rows_of, slots = pieces_of(phase, n)
        arrived(got.at[phase, slots, rows_of], sum_recv.at[phase, n])
        total = part[0, phase, rows_of].astype(F32)
        for k in range(ring[axis] - 1):
            total = total + got[phase, k, rows_of].astype(F32)
        return total

    def start_sum(payload):
        part[0, 0] = payload
        for n in range(2):
            send_piece(0, n)

    def end_sum():
        for n in range(2):
            part[0, 1, pl.ds(PIECES[n][1], PIECES[n][2])] = collect(0, n).astype(BF)
            send_piece(1, n)
        return jnp.concatenate([collect(1, n) for n in range(2)], axis=0)

    def sum_sent():
        for phase in range(2):
            for n in range(2):
                _, rows_of, slots = pieces_of(phase, n)
                arrived(got.at[phase, slots, rows_of], sum_send.at[phase, n])

    def exchange(corr):
        c_own[...] = packed(corr).astype(BF)
        remote(c_own, c_prev, c_send, c_recv.at[0], (r, nxt))
        remote(c_own, c_next, c_send, c_recv.at[1], (r, prv))

    plane = nx * ny
    slots, rest = divmod(SUM // TILE, plane)
    final = part.at[1, 0]
    peer_at = [lax.rem(r + k, plane) for k in range(plane)]

    def tile(n):
        return pl.ds(n * TILE if isinstance(n, int) else pl.multiple_of(n * TILE, TILE), TILE)

    def scatter(payload):
        part[1, 0] = payload
        for j in range(rest):
            n = slots * plane + j

            @pl.when(r != j)
            def _():
                remote(
                    final.at[tile(n)], rest_got.at[lax.rem(r - j + plane, plane) - 1],
                    rest_send.at[j], rest_recv, (j, p),
                )

        for s in range(slots):
            for k in range(1, plane):
                remote(
                    final.at[tile(s * plane + peer_at[k])], tile_got.at[s, k - 1],
                    tile_send, tile_recv, (peer_at[k], p),
                )

    def gather():
        def spread(src, n, send):
            for k in range(plane):
                remote(src, tot_prev.at[tile(n)], send.at[0], tot_recv.at[0], (peer_at[k], nxt))
                remote(src, tot_next.at[tile(n)], send.at[1], tot_recv.at[1], (peer_at[k], prv))

        if slots:
            arrived(tile_got, tile_recv)
        for s in range(slots):
            n = s * plane + r
            total = part[1, 0, tile(n)].astype(F32)
            for k in range(plane - 1):
                total = total + tile_got[s, k].astype(F32)
            sums[s] = total.astype(BF)
            spread(sums.at[s], n, spread_send.at[s])

        @pl.when(r < rest)
        def _():
            n = slots * plane + r
            arrived(rest_got, rest_recv)
            total = part[1, 0, tile(n)].astype(F32)
            for k in range(plane - 1):
                total = total + rest_got[k].astype(F32)
            sums[slots] = total.astype(BF)
            spread(sums.at[slots], n, spread_send.at[slots])

    def gathered():
        for j in range(rest):
            @pl.when(r != j)
            def _():
                arrived(final.at[tile(slots * plane + j)], rest_send.at[j])
        if slots:
            arrived(tile_got, tile_send)
        for s in range(slots):
            for side in range(2):
                arrived(everyone, spread_send.at[s, side])

        @pl.when(r < rest)
        def _():
            for side in range(2):
                arrived(everyone, spread_send.at[slots, side])

    def forward(c):
        remote(in_l.at[c], far_l.at[c], mv_send.at[2], far_recv.at[0], (r, nxt))
        remote(in_r.at[c], far_r.at[c], mv_send.at[3], far_recv.at[1], (r, prv))

    def turn_left(c, src, weights, dst):
        a = dot(src[pl.ds(c * ch, g)], weights[0])
        b = dot(src[pl.ds(c * ch + g, g)], weights[1])
        dst[c, :g] = a[:, :128].astype(BF)
        dst[c, g : 2 * g] = b[:, :128].astype(BF)
        dst[c, 2 * g :] = (a[:, 128:] + b[:, 128:]).astype(BF)

    def turn_right(c, src, weights, dst):
        a = dot(src[pl.ds(c * ch, g)], weights[0])
        b = dot(src[pl.ds(c * ch + g, g)], weights[1])
        dst[c, :g] = a[:, 128:].astype(BF)
        dst[c, g : 2 * g] = b[:, 128:].astype(BF)
        dst[c, 2 * g :] = (a[:, :128] + b[:, :128]).astype(BF)

    early = pl.ds(0, PRE * ch)
    first_loads = -(-PRE * ch // piece)
    for c in range(first_loads):
        loads[c].wait()
    pl.semaphore_wait(barrier, len(peers))
    remote(w.at[early], raw_l, raw_send, raw_recv.at[0], (r, nxt))
    remote(w.at[early], raw_r, raw_send, raw_recv.at[1], (r, prv))

    sq = jnp.zeros((8, WIDE), F32)
    for c in range(LOADS):
        if c >= first_loads:
            loads[c].wait()
        block = w[pl.ds(c * piece, piece)]
        new = dot_tn(block[:, :256], block[:, 128:])[:BLK]
        if c == 0:
            acc[...] = new
        else:
            acc[...] += new
        wide = block.astype(F32)
        sq = sq + jnp.sum((wide * wide).reshape(piece // 8, 8, WIDE), axis=0)
    sq = jnp.sum(sq, axis=0, keepdims=True)
    start_sum(sent_sum(acc[...], sq[:, :256], sq[:, 128:]))
    corr = corr_of(end_sum())
    exchange(corr)
    scale = scale_of(corr)
    keep_left(ql, *left_columns(corr, scale))
    keep_right(qr, *right_columns(corr, scale))

    for c in range(PRE, CHUNKS):
        turn_left(c, w, ql, own_l)
        remote(own_l.at[c], in_l.at[c], mv_send.at[0], in_recv.at[0, c - PRE], (r, nxt))
        turn_right(c, w, qr, own_r)
        remote(own_r.at[c], in_r.at[c], mv_send.at[1], in_recv.at[1, c - PRE], (r, prv))
    arrived(c_prev, c_recv.at[0])
    arrived(c_next, c_recv.at[1])
    corr = unpacked(c_prev[...].astype(F32))
    keep_left(pql, *left_columns(corr, scale_of(corr)))
    corr = unpacked(c_next[...].astype(F32))
    keep_right(nqr, *right_columns(corr, scale_of(corr)))

    sq_l = [jnp.zeros((8, 128), F32), jnp.zeros((8, 128), F32)]
    sq_r = [jnp.zeros((8, 128), F32), jnp.zeros((8, 128), F32)]

    def squares(total, block):
        wide = block.astype(F32)
        wide = wide * wide
        a = jnp.sum(wide[: 2 * g].reshape(2 * g // 8, 8, 128), axis=0)
        b = jnp.sum(wide[2 * g :].reshape(g // 8, 8, 128), axis=0)
        return [total[0] + a, total[1] + b]

    for c in range(CHUNKS):
        if c == 0:
            arrived(raw_l, raw_recv.at[0])
            arrived(raw_r, raw_recv.at[1])
        if c < PRE:
            turn_left(c, raw_l, pql, in_l)
            turn_right(c, raw_r, nqr, in_r)
        else:
            arrived(in_l.at[c], in_recv.at[0, c - PRE])
            arrived(in_r.at[c], in_recv.at[1, c - PRE])
        if c < CHUNKS - LATE:
            forward(c)
        left, right = in_l[c], in_r[c]
        lb, rb = left[2 * g :], right[2 * g :]
        a = jnp.concatenate([left[: 2 * g], jnp.concatenate([lb, rolled(lb)], axis=0)], axis=1)
        b = jnp.concatenate([jnp.concatenate([rb, rolled(rb)], axis=0), right[: 2 * g]], axis=1)
        new = dot_tn(a, b)[:BLK]
        if c == 0:
            acc[...] = new
        else:
            acc[...] += new
        sq_l = squares(sq_l, left)
        sq_r = squares(sq_r, right)

    def folded(total):
        a, b = (jnp.sum(v, axis=0, keepdims=True) for v in total)
        return a, b + rolled(b)

    la, lb = folded(sq_l)
    ra, rb = folded(sq_r)
    scatter(sent_sum(
        acc[...], jnp.concatenate([la, lb], axis=1), jnp.concatenate([rb, ra], axis=1)
    ))
    for c in range(PRE):
        turn_left(c, w, ql, own_l)
        turn_right(c, w, qr, own_r)
    gather()
    for c in range(CHUNKS - LATE, CHUNKS):
        forward(c)
    sum_sent()
    for side in range(2):
        arrived((own_l, own_r)[side].at[pl.ds(PRE, CHUNKS - PRE)], mv_send.at[side])
    arrived(raw, raw_send)
    arrived(c_both, c_send)

    none = jnp.zeros((64, 256), BF)

    def keep_last(ref, top, low):
        top, low = top.astype(BF), low.astype(BF)
        ref[0, :BLK] = top
        ref[0, BLK:256] = none
        ref[1, :128] = top[:128]
        ref[1, 128:192] = none
        ref[1, 192:256] = top[128:]
        ref[0, 256:320] = none
        ref[0, 320:] = low
        ref[1, 256:320] = low[:64]
        ref[1, 320:384] = none
        ref[1, 384:] = low[64:]

    def finish(side, first):
        from_l, from_r = ((far_l, own_r), (own_l, far_r))[side]
        total = (tot_prev, tot_next)[side]
        arrived(total, tot_recv.at[side])
        corr = corr_of(total[...].astype(F32))
        keep_last(wl, *(left_columns, right_columns)[side](corr, scale_of(corr)))
        arrived((far_l, far_r)[side], far_recv.at[side])
        outer = (pl.ds(0, 128), pl.ds(256, 128))[side]
        for c in range(0, CHUNKS, CHUNKS):
            for half in range(2):
                a_of, b_of = pl.ds(half * g, g), pl.ds(2 * g, g)
                terms = jnp.concatenate([
                    jnp.concatenate(
                        [from_l[n, a_of], from_l[n, b_of], from_r[n, b_of], from_r[n, a_of]], axis=1
                    )
                    for n in range(c, c + CHUNKS)
                ], axis=0)
                a = dot(terms, wl[half])
                for n in range(CHUNKS):
                    rows_of = pl.ds((c + n) * ch + half * g, g)
                    pair = a[n * g : n * g + g, :128], a[n * g : n * g + g, 128:]
                    out_v[rows_of, outer] = pair[side].astype(BF)
                    middle = pair[1 - side]
                    if not first:
                        middle = middle + out_v[rows_of, 128:256].astype(F32)
                    out_v[rows_of, 128:256] = middle.astype(BF)

    @pl.when(lax.rem(p, 2) == 0)
    def _():
        finish(1, True)
        finish(0, False)

    @pl.when(lax.rem(p, 2) == 1)
    def _():
        finish(0, True)
        finish(1, False)

    gathered()
    arrived(in_l, mv_send.at[2])
    arrived(in_r, mv_send.at[3])


def local(nx, ny, npos, latent):
    rows = latent.shape[0]
    g = rows // CHUNKS // 2
    plane = nx * ny
    slots, rest = divmod(SUM // TILE, plane)
    block = pltpu.VMEM((CHUNKS, 3 * g, 128), BF)
    return pl.pallas_call(
        functools.partial(kernel, nx, ny, npos),
        out_shape=jax.ShapeDtypeStruct(latent.shape, BF),
        in_specs=[pl.BlockSpec(memory_space=pltpu.HBM)],
        out_specs=pl.BlockSpec(memory_space=pltpu.VMEM),
        scratch_shapes=[
            pltpu.VMEM((rows, WIDE), BF),
            block, block, block, block, block, block,
            pltpu.VMEM((2, PRE * 2 * g, WIDE), BF),
            pltpu.VMEM((2, WIDE, 256), BF),
            pltpu.VMEM((2, WIDE, 256), BF),
            pltpu.VMEM((2, WIDE, 256), BF),
            pltpu.VMEM((2, WIDE, 256), BF),
            pltpu.VMEM((2, 512, 256), BF),
            pltpu.VMEM((BLK, 256), F32),
            pltpu.VMEM((2, 2, SUM, 128), BF),
            pltpu.VMEM((2, max(nx, ny) - 1, SUM, 128), BF),
            pltpu.VMEM((PACK, 128), BF),
            pltpu.VMEM((2, PACK, 128), BF),
            pltpu.VMEM((max(slots, 1), plane - 1, TILE, 128), BF),
            pltpu.VMEM((plane - 1, TILE, 128), BF),
            pltpu.VMEM((slots + 1, TILE, 128), BF),
            pltpu.VMEM((plane, TILE, 128), BF),
            pltpu.VMEM((SUM, 128), BF),
            pltpu.VMEM((SUM, 128), BF),
            pltpu.SemaphoreType.DMA((LOADS,)),
            pltpu.SemaphoreType.DMA((2, len(PIECES))),
            pltpu.SemaphoreType.DMA((2, len(PIECES))),
            pltpu.SemaphoreType.DMA((4,)),
            pltpu.SemaphoreType.DMA((2, CHUNKS - PRE)),
            pltpu.SemaphoreType.DMA((2,)),
            pltpu.SemaphoreType.DMA,
            pltpu.SemaphoreType.DMA((2,)),
            pltpu.SemaphoreType.DMA,
            pltpu.SemaphoreType.DMA((2,)),
            pltpu.SemaphoreType.DMA,
            pltpu.SemaphoreType.DMA,
            pltpu.SemaphoreType.DMA((max(rest, 1),)),
            pltpu.SemaphoreType.DMA,
            pltpu.SemaphoreType.DMA((slots + 1, 2)),
            pltpu.SemaphoreType.DMA((2,)),
        ],
        compiler_params=pltpu.CompilerParams(
            collective_id=0, has_side_effects=True, vmem_limit_bytes=54_000_000
        ),
    )(latent)


def solution(mesh):
    side = math.isqrt(mesh.shape["rows"])
    return jax.shard_map(
        functools.partial(local, side, mesh.shape["rows"] // side, mesh.shape["pairs"]),
        mesh=mesh,
        in_specs=(P("rows", "pairs"),),
        out_specs=P("rows", "pairs"),
        check_vma=False,
    )
```

```python
import functools
import math

import jax
import jax.numpy as jnp
from jax import lax
from jax.experimental import pallas as pl
from jax.experimental.pallas import tpu as pltpu
from jax.sharding import PartitionSpec as P

BF = jnp.bfloat16
F32 = jnp.float32
BLK = 192
WIDE = 2 * BLK
CHUNKS = 8
PRE = 4
PACK = 288
SUM = 320
PIECES = ((0, 0, 144), (1, 144, 160))
LOADS = 4
TILE = 32
LATE = 2
MESH = pl.DeviceIdType.MESH


def polynomial():
    a = 1.5 / math.sqrt(65.0)
    t = a * a
    f = [2.25, -2.4375, 1.6875, -0.5625, 0.0625]
    c = []
    for k in range(5):
        c.append(a * sum(f[n] * math.comb(n, k) * t ** (n - k) for n in range(k, 5)))
    return t, c


def dot(a, b):
    return jnp.dot(a, b, preferred_element_type=F32)


def dot_nt(a, b):
    return lax.dot_general(a, b, (((1,), (1,)), ((), ())), preferred_element_type=F32)


def dot_tn(a, b):
    return lax.dot_general(a, b, (((0,), (0,)), ((), ())), preferred_element_type=F32)


def iota(shape, dim):
    return lax.broadcasted_iota(jnp.int32, shape, dim)


def series(h, c, full, eye):
    hb = h.astype(BF)
    h2 = dot(hb, full(hb))
    rest = c[1] * h + c[2] * h2 + dot(h2.astype(BF), full((c[3] * h + c[4] * h2).astype(BF)))
    return jnp.where(eye, rest + c[0], rest), full(rest.astype(BF))


def below(x):
    return jnp.concatenate([x, jnp.zeros((64, 256), x.dtype)], axis=0)


def above(x):
    return jnp.concatenate([jnp.zeros((64, 256), x.dtype), x], axis=0)


def scale_of(corr):
    square = jnp.sum(jnp.sum(corr * corr, axis=0, keepdims=True), axis=1, keepdims=True)
    return 8.0 * lax.rsqrt(2.0 * square + 1e-12)


def left_columns(corr, scale):
    t, c = polynomial()
    cb = corr.astype(BF)
    row, lane = iota((BLK, 256), 0), iota((BLK, 256), 1)
    ct = below(corr).T[64:]
    q1, p1 = series((t * scale * scale) * dot_nt(cb, below(cb)), c, below, row == lane)
    return q1, -scale * (c[0] * ct + dot(ct.astype(BF), p1))


def right_columns(corr, scale):
    t, c = polynomial()
    cb = corr.astype(BF)
    ctb = below(corr).T[64:].astype(BF)
    row, lane = iota((BLK, 256), 0), iota((BLK, 256), 1)
    q2, p2 = series((t * scale * scale) * dot_nt(ctb, above(ctb)), c, above, row + 64 == lane)
    return scale * (c[0] * corr + dot(cb, p2)), q2


def rolled(x):
    return pltpu.roll(x, 64, axis=1)


def packed(x):
    lane = iota((BLK // 2, 128), 1)
    low, high = x[: BLK // 2, :128], x[BLK // 2 :, :128]
    return jnp.concatenate([x[:, 128:], jnp.where(lane >= 64, low, rolled(high))], axis=0)


def unpacked(x):
    lane = iota((BLK // 2, 128), 1)
    shared = x[BLK:PACK]
    low = jnp.where(lane >= 64, shared, 0.0)
    high = jnp.where(lane >= 64, rolled(shared), 0.0)
    return jnp.concatenate([jnp.concatenate([low, high], axis=0), x[:BLK]], axis=1)


def sent_sum(gram, left_sq, right_sq):
    row = iota((SUM - PACK, 128), 0)
    side = jnp.zeros((SUM - PACK, 128), F32)
    for n, value in enumerate((left_sq[:, :128], left_sq[:, 128:], right_sq[:, :128], right_sq[:, 128:])):
        side = jnp.where(row == n, value, side)
    return jnp.concatenate([packed(gram), side], axis=0).astype(BF)


def corr_of(total):
    gram, n = unpacked(total), total[PACK:]
    row, lane = iota((BLK, 128), 0), iota((BLK, 128), 1)
    left_sq = jnp.where(row < 128, n[0:1], n[1:2])
    left_sq = jnp.where(lane == lax.rem(row, 128), left_sq, 0.0)
    left_sq = jnp.sum(left_sq, axis=1, keepdims=True)
    right_sq = jnp.concatenate([n[2:3], n[3:4]], axis=1)
    corr = gram * lax.rsqrt(left_sq) * lax.rsqrt(right_sq)
    return jnp.where(iota((BLK, 256), 1) >= 64, corr, 0.0)


def keep_left(ref, q1, nkt):
    for rows_of, value in ((pl.ds(0, BLK), q1), (pl.ds(BLK, BLK), nkt)):
        ref[0, rows_of] = value.astype(BF)
        ref[1, rows_of, :128] = value[:, :128].astype(BF)
        ref[1, rows_of, 128:] = rolled(value[:, 128:]).astype(BF)


def keep_right(ref, k, q2):
    for rows_of, value in ((pl.ds(0, BLK), k), (pl.ds(BLK, BLK), q2)):
        ref[0, rows_of] = value.astype(BF)
        ref[1, rows_of, :128] = rolled(value[:, :128]).astype(BF)
        ref[1, rows_of, 128:] = value[:, 128:].astype(BF)


def kernel(
    nx, ny, npos,
    w_hbm, out_v,
    w, own_l, own_r, in_l, in_r, far_l, far_r, raw,
    ql, qr, pql, nqr, wl, acc, part, got, c_own, c_both,
    tile_got, rest_got, sums, everyone, tot_prev, tot_next,
    load_sem, sum_send, sum_recv, mv_send, in_recv, far_recv, c_send, c_recv, raw_send, raw_recv,
    tile_send, tile_recv, rest_send, rest_recv, spread_send, tot_recv,
):
    r, p = lax.axis_index("rows"), lax.axis_index("pairs")
    x, y = lax.rem(r, nx), lax.div(r, nx)
    nxt, prv = lax.rem(p + 1, npos), lax.rem(p + npos - 1, npos)
    rows = w_hbm.shape[0]
    ch = rows // CHUNKS
    g = ch // 2

    def along(axis, k):
        if axis == 0:
            return (y * nx + lax.rem(x + k, nx), p)
        return (lax.rem(y + k, ny) * nx + x, p)

    ring = (nx, ny)
    raw_l, raw_r = raw.at[0], raw.at[1]
    c_prev, c_next = c_both.at[0], c_both.at[1]
    peers = [along(a, k) for a in (0, 1) for k in range(1, ring[a])] + [(r, nxt), (r, prv)]

    piece = rows // LOADS
    loads = [
        pltpu.make_async_copy(
            w_hbm.at[pl.ds(c * piece, piece)], w.at[pl.ds(c * piece, piece)], load_sem.at[c]
        )
        for c in range(LOADS)
    ]
    for copy in loads:
        copy.start()
    barrier = pltpu.get_barrier_semaphore()
    for peer in peers:
        pl.semaphore_signal(barrier, inc=1, device_id=peer, device_id_type=MESH)

    def remote(src, dst, send, recv, target):
        pltpu.make_async_remote_copy(
            src_ref=src, dst_ref=dst, send_sem=send, recv_sem=recv,
            device_id=target, device_id_type=MESH,
        ).start()

    def arrived(ref, sem):
        pltpu.make_async_copy(ref, ref, sem).wait()

    def pieces_of(phase, n):
        first, start, size = PIECES[n]
        axis = (phase + first) % 2
        return axis, pl.ds(start, size), pl.ds(0, ring[axis] - 1)

    def send_piece(phase, n):
        axis, rows_of, _ = pieces_of(phase, n)
        for k in (2, 1, 3):
            if k < ring[axis]:
                remote(
                    part.at[0, phase, rows_of], got.at[phase, k - 1, rows_of],
                    sum_send.at[phase, n], sum_recv.at[phase, n], along(axis, k),
                )

    def collect(phase, n):
        axis, rows_of, slots = pieces_of(phase, n)
        arrived(got.at[phase, slots, rows_of], sum_recv.at[phase, n])
        total = part[0, phase, rows_of].astype(F32)
        for k in range(ring[axis] - 1):
            total = total + got[phase, k, rows_of].astype(F32)
        return total

    def start_sum(payload):
        part[0, 0] = payload
        for n in range(2):
            send_piece(0, n)

    def end_sum():
        for n in range(2):
            part[0, 1, pl.ds(PIECES[n][1], PIECES[n][2])] = collect(0, n).astype(BF)
            send_piece(1, n)
        return jnp.concatenate([collect(1, n) for n in range(2)], axis=0)

    def sum_sent():
        for phase in range(2):
            for n in range(2):
                _, rows_of, slots = pieces_of(phase, n)
                arrived(got.at[phase, slots, rows_of], sum_send.at[phase, n])

    def exchange(corr):
        c_own[...] = packed(corr).astype(BF)
        remote(c_own, c_prev, c_send, c_recv.at[0], (r, nxt))
        remote(c_own, c_next, c_send, c_recv.at[1], (r, prv))

    plane = nx * ny
    slots, rest = divmod(SUM // TILE, plane)
    final = part.at[1, 0]
    peer_at = [lax.rem(r + k, plane) for k in range(plane)]

    def tile(n):
        return pl.ds(n * TILE if isinstance(n, int) else pl.multiple_of(n * TILE, TILE), TILE)

    def scatter(payload):
        part[1, 0] = payload
        for j in range(rest):
            n = slots * plane + j

            @pl.when(r != j)
            def _():
                remote(
                    final.at[tile(n)], rest_got.at[lax.rem(r - j + plane, plane) - 1],
                    rest_send.at[j], rest_recv, (j, p),
                )

        for s in range(slots):
            for k in range(1, plane):
                remote(
                    final.at[tile(s * plane + peer_at[k])], tile_got.at[s, k - 1],
                    tile_send, tile_recv, (peer_at[k], p),
                )

    def gather():
        def spread(src, n, send):
            for k in range(plane):
                remote(src, tot_prev.at[tile(n)], send.at[0], tot_recv.at[0], (peer_at[k], nxt))
            for k in range(plane):
                remote(src, tot_next.at[tile(n)], send.at[1], tot_recv.at[1], (peer_at[k], prv))

        if slots:
            arrived(tile_got, tile_recv)
        for s in range(slots):
            n = s * plane + r
            total = part[1, 0, tile(n)].astype(F32)
            for k in range(plane - 1):
                total = total + tile_got[s, k].astype(F32)
            sums[s] = total.astype(BF)
            spread(sums.at[s], n, spread_send.at[s])

        @pl.when(r < rest)
        def _():
            n = slots * plane + r
            arrived(rest_got, rest_recv)
            total = part[1, 0, tile(n)].astype(F32)
            for k in range(plane - 1):
                total = total + rest_got[k].astype(F32)
            sums[slots] = total.astype(BF)
            spread(sums.at[slots], n, spread_send.at[slots])

    def gathered():
        for j in range(rest):
            @pl.when(r != j)
            def _():
                arrived(final.at[tile(slots * plane + j)], rest_send.at[j])
        if slots:
            arrived(tile_got, tile_send)
        for s in range(slots):
            for side in range(2):
                arrived(everyone, spread_send.at[s, side])

        @pl.when(r < rest)
        def _():
            for side in range(2):
                arrived(everyone, spread_send.at[slots, side])

    def forward(c):
        remote(in_l.at[c], far_l.at[c], mv_send.at[2], far_recv.at[0], (r, nxt))
        remote(in_r.at[c], far_r.at[c], mv_send.at[3], far_recv.at[1], (r, prv))

    def turn_left(c, src, weights, dst):
        a = dot(src[pl.ds(c * ch, g)], weights[0])
        b = dot(src[pl.ds(c * ch + g, g)], weights[1])
        dst[c, :g] = a[:, :128].astype(BF)
        dst[c, g : 2 * g] = b[:, :128].astype(BF)
        dst[c, 2 * g :] = (a[:, 128:] + b[:, 128:]).astype(BF)

    def turn_right(c, src, weights, dst):
        a = dot(src[pl.ds(c * ch, g)], weights[0])
        b = dot(src[pl.ds(c * ch + g, g)], weights[1])
        dst[c, :g] = a[:, 128:].astype(BF)
        dst[c, g : 2 * g] = b[:, 128:].astype(BF)
        dst[c, 2 * g :] = (a[:, :128] + b[:, :128]).astype(BF)

    early = pl.ds(0, PRE * ch)
    first_loads = -(-PRE * ch // piece)
    for c in range(first_loads):
        loads[c].wait()
    pl.semaphore_wait(barrier, len(peers))
    remote(w.at[early], raw_l, raw_send, raw_recv.at[0], (r, nxt))
    remote(w.at[early], raw_r, raw_send, raw_recv.at[1], (r, prv))

    sq = jnp.zeros((8, WIDE), F32)
    for c in range(LOADS):
        if c >= first_loads:
            loads[c].wait()
        block = w[pl.ds(c * piece, piece)]
        new = dot_tn(block[:, :256], block[:, 128:])[:BLK]
        if c == 0:
            acc[...] = new
        else:
            acc[...] += new
        wide = block.astype(F32)
        sq = sq + jnp.sum((wide * wide).reshape(piece // 8, 8, WIDE), axis=0)
    sq = jnp.sum(sq, axis=0, keepdims=True)
    start_sum(sent_sum(acc[...], sq[:, :256], sq[:, 128:]))
    corr = corr_of(end_sum())
    exchange(corr)
    scale = scale_of(corr)
    keep_left(ql, *left_columns(corr, scale))
    keep_right(qr, *right_columns(corr, scale))

    for c in range(PRE, CHUNKS):
        turn_left(c, w, ql, own_l)
        remote(own_l.at[c], in_l.at[c], mv_send.at[0], in_recv.at[0, c - PRE], (r, nxt))
        turn_right(c, w, qr, own_r)
        remote(own_r.at[c], in_r.at[c], mv_send.at[1], in_recv.at[1, c - PRE], (r, prv))
    arrived(c_prev, c_recv.at[0])
    arrived(c_next, c_recv.at[1])
    corr = unpacked(c_prev[...].astype(F32))
    keep_left(pql, *left_columns(corr, scale_of(corr)))
    corr = unpacked(c_next[...].astype(F32))
    keep_right(nqr, *right_columns(corr, scale_of(corr)))

    sq_l = [jnp.zeros((8, 128), F32), jnp.zeros((8, 128), F32)]
    sq_r = [jnp.zeros((8, 128), F32), jnp.zeros((8, 128), F32)]

    def squares(total, block):
        wide = block.astype(F32)
        wide = wide * wide
        a = jnp.sum(wide[: 2 * g].reshape(2 * g // 8, 8, 128), axis=0)
        b = jnp.sum(wide[2 * g :].reshape(g // 8, 8, 128), axis=0)
        return [total[0] + a, total[1] + b]

    for c in range(CHUNKS):
        if c == 0:
            arrived(raw_l, raw_recv.at[0])
            arrived(raw_r, raw_recv.at[1])
        if c < PRE:
            turn_left(c, raw_l, pql, in_l)
            turn_right(c, raw_r, nqr, in_r)
        else:
            arrived(in_l.at[c], in_recv.at[0, c - PRE])
            arrived(in_r.at[c], in_recv.at[1, c - PRE])
        if c < CHUNKS - LATE:
            forward(c)
        left, right = in_l[c], in_r[c]
        lb, rb = left[2 * g :], right[2 * g :]
        a = jnp.concatenate([left[: 2 * g], jnp.concatenate([lb, rolled(lb)], axis=0)], axis=1)
        b = jnp.concatenate([jnp.concatenate([rb, rolled(rb)], axis=0), right[: 2 * g]], axis=1)
        new = dot_tn(a, b)[:BLK]
        if c == 0:
            acc[...] = new
        else:
            acc[...] += new
        sq_l = squares(sq_l, left)
        sq_r = squares(sq_r, right)

    def folded(total):
        a, b = (jnp.sum(v, axis=0, keepdims=True) for v in total)
        return a, b + rolled(b)

    la, lb = folded(sq_l)
    ra, rb = folded(sq_r)
    scatter(sent_sum(
        acc[...], jnp.concatenate([la, lb], axis=1), jnp.concatenate([rb, ra], axis=1)
    ))
    for c in range(PRE):
        turn_left(c, w, ql, own_l)
        turn_right(c, w, qr, own_r)
    gather()
    for c in range(CHUNKS - LATE, CHUNKS):
        forward(c)
    sum_sent()
    for side in range(2):
        arrived((own_l, own_r)[side].at[pl.ds(PRE, CHUNKS - PRE)], mv_send.at[side])
    arrived(raw, raw_send)
    arrived(c_both, c_send)

    none = jnp.zeros((64, 256), BF)

    def keep_last(ref, top, low):
        top, low = top.astype(BF), low.astype(BF)
        ref[0, :BLK] = top
        ref[0, BLK:256] = none
        ref[1, :128] = top[:128]
        ref[1, 128:192] = none
        ref[1, 192:256] = top[128:]
        ref[0, 256:320] = none
        ref[0, 320:] = low
        ref[1, 256:320] = low[:64]
        ref[1, 320:384] = none
        ref[1, 384:] = low[64:]

    def finish(side, first):
        from_l, from_r = ((far_l, own_r), (own_l, far_r))[side]
        total = (tot_prev, tot_next)[side]
        arrived(total, tot_recv.at[side])
        corr = corr_of(total[...].astype(F32))
        keep_last(wl, *(left_columns, right_columns)[side](corr, scale_of(corr)))
        arrived((far_l, far_r)[side], far_recv.at[side])
        outer = (pl.ds(0, 128), pl.ds(256, 128))[side]
        for c in range(0, CHUNKS, CHUNKS):
            for half in range(2):
                a_of, b_of = pl.ds(half * g, g), pl.ds(2 * g, g)
                terms = jnp.concatenate([
                    jnp.concatenate(
                        [from_l[n, a_of], from_l[n, b_of], from_r[n, b_of], from_r[n, a_of]], axis=1
                    )
                    for n in range(c, c + CHUNKS)
                ], axis=0)
                a = dot(terms, wl[half])
                for n in range(CHUNKS):
                    rows_of = pl.ds((c + n) * ch + half * g, g)
                    pair = a[n * g : n * g + g, :128], a[n * g : n * g + g, 128:]
                    out_v[rows_of, outer] = pair[side].astype(BF)
                    middle = pair[1 - side]
                    if not first:
                        middle = middle + out_v[rows_of, 128:256].astype(F32)
                    out_v[rows_of, 128:256] = middle.astype(BF)

    @pl.when(lax.rem(p, 2) == 0)
    def _():
        finish(1, True)
        finish(0, False)

    @pl.when(lax.rem(p, 2) == 1)
    def _():
        finish(0, True)
        finish(1, False)

    gathered()
    arrived(in_l, mv_send.at[2])
    arrived(in_r, mv_send.at[3])


def local(nx, ny, npos, latent):
    rows = latent.shape[0]
    g = rows // CHUNKS // 2
    plane = nx * ny
    slots, rest = divmod(SUM // TILE, plane)
    block = pltpu.VMEM((CHUNKS, 3 * g, 128), BF)
    return pl.pallas_call(
        functools.partial(kernel, nx, ny, npos),
        out_shape=jax.ShapeDtypeStruct(latent.shape, BF),
        in_specs=[pl.BlockSpec(memory_space=pltpu.HBM)],
        out_specs=pl.BlockSpec(memory_space=pltpu.VMEM),
        scratch_shapes=[
            pltpu.VMEM((rows, WIDE), BF),
            block, block, block, block, block, block,
            pltpu.VMEM((2, PRE * 2 * g, WIDE), BF),
            pltpu.VMEM((2, WIDE, 256), BF),
            pltpu.VMEM((2, WIDE, 256), BF),
            pltpu.VMEM((2, WIDE, 256), BF),
            pltpu.VMEM((2, WIDE, 256), BF),
            pltpu.VMEM((2, 512, 256), BF),
            pltpu.VMEM((BLK, 256), F32),
            pltpu.VMEM((2, 2, SUM, 128), BF),
            pltpu.VMEM((2, max(nx, ny) - 1, SUM, 128), BF),
            pltpu.VMEM((PACK, 128), BF),
            pltpu.VMEM((2, PACK, 128), BF),
            pltpu.VMEM((max(slots, 1), plane - 1, TILE, 128), BF),
            pltpu.VMEM((plane - 1, TILE, 128), BF),
            pltpu.VMEM((slots + 1, TILE, 128), BF),
            pltpu.VMEM((plane, TILE, 128), BF),
            pltpu.VMEM((SUM, 128), BF),
            pltpu.VMEM((SUM, 128), BF),
            pltpu.SemaphoreType.DMA((LOADS,)),
            pltpu.SemaphoreType.DMA((2, len(PIECES))),
            pltpu.SemaphoreType.DMA((2, len(PIECES))),
            pltpu.SemaphoreType.DMA((4,)),
            pltpu.SemaphoreType.DMA((2, CHUNKS - PRE)),
            pltpu.SemaphoreType.DMA((2,)),
            pltpu.SemaphoreType.DMA,
            pltpu.SemaphoreType.DMA((2,)),
            pltpu.SemaphoreType.DMA,
            pltpu.SemaphoreType.DMA((2,)),
            pltpu.SemaphoreType.DMA,
            pltpu.SemaphoreType.DMA,
            pltpu.SemaphoreType.DMA((max(rest, 1),)),
            pltpu.SemaphoreType.DMA,
            pltpu.SemaphoreType.DMA((slots + 1, 2)),
            pltpu.SemaphoreType.DMA((2,)),
        ],
        compiler_params=pltpu.CompilerParams(
            collective_id=0, has_side_effects=True, vmem_limit_bytes=54_000_000
        ),
    )(latent)


def solution(mesh):
    side = math.isqrt(mesh.shape["rows"])
    return jax.shard_map(
        functools.partial(local, side, mesh.shape["rows"] // side, mesh.shape["pairs"]),
        mesh=mesh,
        in_specs=(P("rows", "pairs"),),
        out_specs=P("rows", "pairs"),
        check_vma=False,
    )
```
